256 devices in a mesh: gen: 32 (over z, y_lo, core), neur: 4 (over x), box: 2 (over y_hi).
Axes of the slice: x: 4, y: 4 (y_hi: 2, y_lo: 2; y = y_hi * 2 + y_lo), z: 8, core: 2. Of those that a mesh axis runs over, the one named last changes fastest.
Arguments:
- gens: bfloat16 [8, 1024, 4096], P('box', 'gen'), may hold values from -1 to 1
- center: bfloat16 [8, 4096], P('box'), may hold values from -6 to 6
- weight: bfloat16 [4096, 2048], P('gen', 'neur'), may hold values from -0.09375 to 0.09375
- bias: float32 [2048], P('neur'), may hold values from -3 to 3
- phase: int32 [8, 2048], P('box', 'neur'), may hold values from 0 to 2
- gens_cot: bfloat16 [8, 1024, 2048], P('box', 'gen', 'neur'), may hold values from -6 to 6
- center_cot: float32 [8, 2048], P('box', 'neur'), may hold values from -6 to 6
- offset_cot: float32 [8, 2048], P('box', 'neur'), may hold values from -6 to 6
Outputs:
- center_out: float32 [8, 2048], P('box', 'neur')
- gens_out: bfloat16 [8, 1024, 2048], P('box', 'gen', 'neur')
- offset: float32 [8, 2048], P('box', 'neur')
- weight_grad: float32 [4096, 2048], P('gen', 'neur')
- bias_grad: float32 [2048], P('neur')
- gens_grad: float32 [8, 1024, 4096], P('box', 'gen', 'neur')
- center_grad: float32 [8, 4096], P('box', 'neur')
The draws below stay inside these ranges and needn't reach their ends.
Inputs may be any that keep to these rules, and one draw needn't show every extreme that they name: `phase`: 0 marks an inactive neuron, 1 an active one, 2 one that crosses zero.
All inputs are finite; a program needn't handle non-finite values.
Results may differ from the reference program's by a relative error of at most 0.006.
Values may be sent and summed in bfloat16 or wider, within the bound.
A program may use at most 64 MiB of HBM per device.

```python
import math
import jax
import jax.numpy as jnp
from jax import lax

D = 4096
F = 2048
BOXES = 8
GENS = 1024


def draw_gens(key, part):
    keys = jax.random.split(key, 3)
    index = jnp.arange(GENS, dtype=jnp.float32)
    rising = 1.0 + 2.0 * index / max(GENS - 1, 1)
    row_scale = jnp.exp(jax.random.uniform(keys[0], (BOXES, GENS, 1), minval=0.0, maxval=math.log(10.0)))
    col_scale = jnp.exp(jax.random.uniform(keys[1], (1, 1, D), minval=-1.15, maxval=1.15))
    base = jnp.clip(jax.random.normal(keys[2], (BOXES, GENS, D)), -4.0, 4.0)
    value = base * row_scale * col_scale * rising[None, :, None] / (6.0 * GENS)
    return jnp.clip(value, -1.0, 1.0).astype(jnp.bfloat16)


def plant(entries, key, smallest, largest):
    longest = entries.shape.index(max(entries.shape))
    spots = []
    for shift in (0, 1):
        where = [jax.random.randint(jax.random.fold_in(key, axis), (), 0, length) for axis, length in enumerate(entries.shape)]
        where[longest] = (where[longest] + shift) % entries.shape[longest]
        spots.append(tuple(where))
    return entries.at[spots[0]].set(smallest).at[spots[1]].set(largest)


def block_levels(stream_key, extent, cuts, low, top_value):
    def one(axis_at, blocks):
        draws = jax.random.uniform(jax.random.fold_in(jax.random.fold_in(stream_key, 6), axis_at), (blocks,), jnp.float32, low / len(cuts), top_value / len(cuts))
        return jnp.repeat(jnp.exp(draws), extent[axis_at] // blocks).reshape((-1,) + (1,) * (len(extent) - axis_at - 1))

    loudness = one(*cuts[0])
    for cut in cuts[1:]:
        loudness = loudness * one(*cut)
    return loudness


def normal_values(rng, shape, spread, bound, shards=(), kind=jnp.bfloat16):
    drawn = jax.random.normal(rng, shape, jnp.float32) * spread
    if len(shards) > 0:
        drawn = block_levels(rng, shape, shards, -0.22, 0.18) * drawn
    return jnp.clip(drawn, min=-bound, max=bound).astype(kind)


def setup_inputs(seed: int = 0) -> dict:
    seeds = jax.random.split(jax.random.key(seed), 9)
    gens = draw_gens(jax.random.fold_in(seeds[8], 71), 0)
    center = normal_values(seeds[1], (BOXES, D), 1.0, 6.0, ((0, 2),))
    weight = normal_values(seeds[2], (D, F), D ** -0.5, 0.09375, ((0, 32), (1, 4)))
    bias = normal_values(seeds[3], (F,), 0.5, 3.0, ((0, 4),), jnp.float32)
    phase = plant(jax.random.randint(seeds[4], (BOXES, F), 0, 3), jax.random.fold_in(seeds[4], 1), 0, 2).astype(jnp.int32)
    gens_cot = normal_values(seeds[5], (BOXES, GENS, F), 1.0, 6.0, ((0, 2), (1, 32), (2, 4)))
    center_cot = normal_values(seeds[6], (BOXES, F), 1.0, 6.0, ((0, 2), (1, 4)), jnp.float32)
    offset_cot = normal_values(seeds[7], (BOXES, F), 1.0, 6.0, ((0, 2), (1, 4)), jnp.float32)
    return {"gens": gens, "center": center, "weight": weight, "bias": bias, "phase": phase, "gens_cot": gens_cot, "center_cot": center_cot, "offset_cot": offset_cot}


def neuron(center_pre, radius, phase):
    upper = center_pre + radius
    lower = center_pre - radius
    ratio = jnp.clip(upper / (upper - lower + 1e-05), 0.0, 1.0)
    active = (phase == 1).astype(center_pre.dtype)
    crossing = (phase == 2).astype(center_pre.dtype)
    slope = active + crossing * ratio
    offset = crossing * (-ratio * lower * 0.5)
    return (slope, slope * center_pre + offset, offset)

def reference(gens, center, weight, bias, phase, gens_cot, center_cot, offset_cot):
    total_rows = BOXES * GENS
    wide = jnp.concatenate([gens.reshape(total_rows, D), center], 0)
    product = jnp.dot(wide, weight, preferred_element_type=jnp.float32)
    gen_pre = product[:total_rows].reshape(BOXES, GENS, F)
    center_pre = product[total_rows:] + bias
    radius = lax.optimization_barrier(jnp.sum(jnp.abs(gen_pre), axis=1))
    slope, center_out, offset = neuron(center_pre, radius, phase)
    gens_out = (slope[:, None, :] * gen_pre).astype(jnp.bfloat16)
    intersection = lax.optimization_barrier(jnp.sum(gens_cot.astype(jnp.float32) * gen_pre, axis=1))
    unused, pull = jax.vjp(lambda a, b: neuron(a, b, phase), center_pre, radius)
    g_center, g_radius = pull((intersection, center_cot, offset_cot))
    gen_back = (slope[:, None, :] * gens_cot.astype(jnp.float32) + jnp.sign(gen_pre) * g_radius[:, None, :]).astype(jnp.bfloat16)
    center_back = g_center.astype(jnp.bfloat16)
    back = jnp.concatenate([gen_back.reshape(total_rows, F), center_back], 0)
    weight_grad = jnp.dot(wide.T, back, preferred_element_type=jnp.float32)
    bias_grad = lax.optimization_barrier(jnp.sum(g_center, axis=0))
    input_back = jnp.dot(back, weight.T, preferred_element_type=jnp.float32)
    gens_grad = input_back[:total_rows].reshape(BOXES, GENS, D)
    center_grad = input_back[total_rows:]
    return (center_out, gens_out, offset, weight_grad, bias_grad, gens_grad, center_grad)
```

```python
import functools

import jax
import jax.numpy as jnp
from jax import lax
from jax.experimental import pallas as pl
from jax.experimental.pallas import tpu as pltpu
from jax.sharding import PartitionSpec as P

MESH = pl.DeviceIdType.MESH
F32 = jnp.float32
BF16 = jnp.bfloat16

NZ = 8
D = 4096
COLS = 512
ROWS = 128
WIDE = 144


def neuron(center_pre, radius, phase):
    upper = center_pre + radius
    lower = center_pre - radius
    ratio = jnp.clip(upper / (upper - lower + 1e-05), 0.0, 1.0)
    active = (phase == 1).astype(center_pre.dtype)
    crossing = (phase == 2).astype(center_pre.dtype)
    slope = active + crossing * ratio
    offset = crossing * (-ratio * lower * 0.5)
    return (slope, slope * center_pre + offset, offset)


def copy_to(src, dst, send_sem, recv_sem, device):
    return pltpu.make_async_remote_copy(
        src_ref=src,
        dst_ref=dst,
        send_sem=send_sem,
        recv_sem=recv_sem,
        device_id=device,
        device_id_type=MESH,
    )


def zsteps(d):
    return {0: (0,), 4: (4,)}.get(d, (-d, d))


def kernel(
    gens_hbm, center_ref, w_hbm, bias_ref, phase_ref, cot_ref, ccot_ref, ocot_ref,
    cout_ref, gout_ref, off_ref, wg_ref, bg_ref, gg_ref, cg_ref,
    w, wide, acc, cslot, gt, amat, sa, sb, bk, bmat, cmat, zs, zr, gs, gr, fx, xb,
    load_sem, w_send, w_recv, a_send, a_recv, ax_send, ax_recv,
    sa_send, sa_recv, sb_send, sb_recv, b_send, b_recv, bp_send,
    g_send, g_recv, z_send, z_recv, f_send, f_recv, x_send, x_recv,
):
    me = lax.axis_index("gen")
    x = lax.axis_index("neur")
    yhi = lax.axis_index("box")
    z = me // 4
    ylo = (me // 2) % 2
    c = me % 2
    y = yhi * 2 + ylo
    quad = ylo * 2 + c

    def dev(zz, yy, cc, xx=None):
        return (zz * 4 + (yy % 2) * 2 + cc, x if xx is None else xx, yy // 2)

    def zdev(k):
        return dev((z + NZ + k) % NZ, y, c)

    def ydev(k, cc=None):
        return dev(z, (y + k) % 4, c if cc is None else cc)

    def xdev(k):
        return dev(z, y, c, (x + k) % 4)

    partner = dev(z, y, 1 - c)
    other_box = ydev(2)

    load_w = pltpu.make_async_copy(w_hbm, w.at[pl.ds(pl.multiple_of(me * 128, 128), 128)], load_sem.at[0])
    load_g = pltpu.make_async_copy(gens_hbm, wide.at[pl.ds(0, ROWS)], load_sem.at[1])
    load_w.start()
    load_g.start()

    barrier = pltpu.get_barrier_semaphore()
    peers = [partner] + [zdev(k) for k in range(1, NZ)] + [xdev(k) for k in (1, 2, 3)]
    peers += [ydev(k, cc) for k in (1, 2, 3) for cc in (0, 1)]
    for peer in peers:
        pl.semaphore_signal(barrier, inc=1, device_id=peer, device_id_type=MESH)

    wide[pl.ds(ROWS, 16)] = jnp.concatenate([center_ref[...].astype(F32), jnp.zeros((12, D), F32)], 0).astype(BF16)
    acc[...] = jnp.zeros_like(acc)
    bk[pl.ds(ROWS, 16)] = jnp.zeros((16, COLS), BF16)
    load_w.wait()
    load_g.wait()
    pl.semaphore_wait(barrier, len(peers))

    def half(zz, yl, cc, h):
        g = zz * 4 + yl * 2 + cc
        return w.at[pl.ds(pl.multiple_of(g * 128 + h * 64, 64), 64)], g * 2 + h

    def wcopy(kind, zz, yl, cc, h):
        ref, at = half(zz, yl, cc, h)
        if kind == 2:
            to = ydev(1) if h == 0 else ydev(3)
        else:
            to = (zdev(1), zdev(-1), None, partner)[kind]
        return copy_to(ref, ref, w_send.at[kind, at], w_recv.at[at], to)

    sent = []

    def send(kind, zz, yl, cc, h):
        cp = wcopy(kind, zz, yl, cc, h)
        cp.start()
        sent.append(cp)

    def arrived(zz, yl, cc, h):
        wcopy(3, zz, yl, cc, h).wait_recv()

    for h in (0, 1):
        send(0, z, ylo, c, h)
        send(1, z, ylo, c, 1 - h)
    for h in (0, 1):
        send(2, z, ylo, c, h)
    for h in (0, 1):
        send(3, z, ylo, c, h)

    def turn(i, carry):
        at = pl.multiple_of(i * 128, 128)
        gt[pl.ds(at, 128), :] = wide[0:ROWS, pl.ds(at, 128)].astype(F32).T.astype(BF16)
        return carry

    lax.fori_loop(0, D // 128, turn, 0)
    gt3 = gt.reshape(NZ, 512, 128)

    def a_rows(yy, cc):
        return pl.ds(pl.multiple_of((yy % 2) * 256 + cc * 128 + (yy // 2) * 64, 64), 64)

    def lanes(at, n=128):
        return pl.ds(pl.multiple_of(at, 128), n)

    mine = pl.ds(2 * x, 2)
    a_sent = []
    for k in (1, 3, 2):
        r = 4 - k
        for cc in (0, 1):
            cp = copy_to(
                gt3.at[mine, a_rows((y + k) % 4, cc), :],
                amat.at[mine, :, lanes((r * 2 + c) * 128)],
                a_send.at[k * 2 + cc],
                a_recv.at[r * 2 + c],
                ydev(k, cc),
            )
            cp.start()
            a_sent.append(cp)
    cp = copy_to(gt3.at[:, a_rows(y, 1 - c), :], amat.at[:, :, lanes(c * 128)], a_send.at[0], a_recv.at[c], partner)
    cp.start()
    a_sent.append(cp)
    own_a = pltpu.make_async_copy(gt3.at[:, a_rows(y, c), :], amat.at[:, :, lanes(c * 128)], load_sem.at[2])
    own_a.start()

    def a_spread():
        for r in (1, 2, 3):
            for cc in (0, 1):
                ref = amat.at[mine, :, lanes((r * 2 + cc) * 128)]
                copy_to(ref, ref, a_send.at[1], a_recv.at[r * 2 + cc], partner).wait_recv()
        ref = amat.at[mine, :, lanes(256, 768)]
        for k in (2, 1, 3):
            cp = copy_to(ref, ref, ax_send.at[k - 1], ax_recv.at[3 - k], xdev(k))
            cp.start()
            a_sent.append(cp)

    def handle_y(d):
        for dz in zsteps(d):
            zz = (z + NZ + dz) % NZ
            for h in (0, 1):
                arrived(zz, 1 - ylo, c, h)
                send(3, zz, 1 - ylo, c, h)

    def compute(d):
        for dz in zsteps(d):
            zz = (z + NZ + dz) % NZ
            for yl in (0, 1):
                for h in (0, 1):
                    arrived(zz, yl, 1 - c, h)
            at = pl.ds(pl.multiple_of(zz * 512, 512), 512)
            res = jnp.dot(wide[:, at], w[at, :], preferred_element_type=F32)
            acc[...] += res[:ROWS]
            cslot[zz] = res[ROWS : ROWS + 8]

    for d in (1, 2, 3, 4):
        for h in (0, 1):
            for way in (0, 1):
                hh = h if way == 0 else 1 - h
                if d == 4 and hh != way:
                    continue
                zz = (z + NZ - d) % NZ if way == 0 else (z + d) % NZ
                arrived(zz, ylo, c, hh)
                if d < 3 or (d == 3 and hh == way):
                    send(way, zz, ylo, c, hh)
                send(2, zz, ylo, c, hh)
                send(3, zz, ylo, c, hh)
        handle_y(d - 1)
        if d == 2:
            a_spread()
        if d >= 2:
            compute(d - 2)
    handle_y(4)
    compute(3)
    compute(4)

    gen_pre = acc[...]
    cot = cot_ref[...].astype(F32)
    part_radius = jnp.sum(jnp.abs(gen_pre).reshape(4, 32, COLS), axis=1)
    part_inner = jnp.sum((cot * gen_pre).reshape(4, 32, COLS), axis=1)
    sa[quad] = jnp.concatenate([part_radius, part_inner], 0)
    for k in (1, 2, 3):
        q = (quad + k) % 4
        cp = copy_to(sa.at[quad], sa.at[quad], sa_send.at[k], sa_recv.at[quad], (z * 4 + q, x, yhi))
        cp.start()
        sent.append(cp)
    for k in (1, 2, 3):
        q = (quad + k) % 4
        copy_to(sa.at[q], sa.at[q], sa_send.at[0], sa_recv.at[q], partner).wait_recv()
    sb[z] = (sa[0] + sa[1]) + (sa[2] + sa[3])
    for k in (4, 3, 5, 2, 6, 1, 7):
        cp = copy_to(sb.at[z], sb.at[z], sb_send.at[k], sb_recv.at[z], zdev(k))
        cp.start()
        sent.append(cp)
    center_pre = cslot[0][0:4]
    for i in range(1, NZ):
        center_pre = center_pre + cslot[i][0:4]
    center_pre = center_pre + bias_ref[...]
    for k in (1, 7, 2, 6, 3, 5, 4):
        zz = (z + k) % NZ
        copy_to(sb.at[zz], sb.at[zz], sb_send.at[0], sb_recv.at[zz], partner).wait_recv()
    total = ((sb[0] + sb[1]) + (sb[2] + sb[3])) + ((sb[4] + sb[5]) + (sb[6] + sb[7]))
    radius = total[0:4]
    intersection = total[4:8]

    phase = phase_ref[...]
    (slope, center_out, offset), pull = jax.vjp(lambda a, b: neuron(a, b, phase), center_pre, radius)
    g_center, g_radius = pull((intersection, ccot_ref[...], ocot_ref[...]))
    pre3 = gen_pre.reshape(4, 32, COLS)
    sign = jnp.where(pre3 > 0, 1.0, jnp.where(pre3 < 0, -1.0, 0.0))
    back = (slope[:, None, :] * cot.reshape(4, 32, COLS) + sign * g_radius[:, None, :]).astype(BF16).reshape(ROWS, COLS)
    bk[0:ROWS] = back
    own_b = pl.multiple_of(c * 128, 128)
    bmat[pl.ds(own_b, 128)] = back

    def b_ref(r, cc, h):
        return bmat.at[pl.ds(pl.multiple_of((r * 2 + cc) * 128 + h * 64, 64), 64)]

    def b_copy(src, r, cc, h, ssem, to):
        return copy_to(src, b_ref(r, cc, h), ssem, b_recv.at[(r * 2 + cc) * 2 + h], to)

    b_sent = []

    def b_start(cp):
        cp.start()
        b_sent.append(cp)

    for i in (0, 1):
        b_start(b_copy(bk.at[i * 64 : i * 64 + 64], 3, c, i, b_send.at[0, i], ydev(1)))
        j = 1 - i
        b_start(b_copy(bk.at[j * 64 : j * 64 + 64], 1, c, j, b_send.at[1, j], ydev(3)))
    for i in (0, 1):
        b_start(b_copy(bk.at[i * 64 : i * 64 + 64], 0, c, i, b_send.at[2, i], partner))

    center_back = g_center.astype(BF16).astype(F32)
    bk[pl.ds(ROWS, 16)] = jnp.concatenate([center_back, jnp.zeros((12, COLS), F32)], 0).astype(BF16)
    xb[yhi, :, 0:COLS] = jnp.concatenate([center_back, jnp.sum(g_center, axis=0, keepdims=True), jnp.zeros((3, COLS), F32)], 0)
    xb[yhi, :, COLS : COLS + 128] = jnp.concatenate(
        [center_ref[:, lanes(me * 128)].astype(F32), jnp.zeros((4, 128), F32)], 0
    )
    xcp = copy_to(xb.at[yhi], xb.at[yhi], x_send, x_recv, other_box)
    xcp.start()
    cout_ref[...] = center_out
    off_ref[...] = offset
    gout_ref[...] = (slope[:, None, :] * pre3).astype(BF16).reshape(ROWS, COLS)

    def partial(k):
        at = pl.ds(pl.multiple_of(((x + k) % 4) * 1024, 1024), 1024)
        return lax.dot_general(bk[...], w[at, :], (((1,), (1,)), ((), ())), preferred_element_type=F32)

    g_sent = []

    def g_start(k):
        gs[k - 1] = partial(k).astype(BF16)
        cp = copy_to(gs.at[k - 1], gr.at[3 - k], g_send.at[k - 1], g_recv.at[3 - k], xdev(k))
        cp.start()
        g_sent.append(cp)

    def b_arrived(r, cc, h):
        b_copy(b_ref(r, cc, h), r, cc, h, b_send.at[0, 0], partner).wait_recv()

    own_a.wait()
    for r in (1, 2, 3):
        ref = amat.at[mine, :, lanes(256, 768)]
        copy_to(ref, ref, ax_send.at[0], ax_recv.at[r - 1], partner).wait_recv()
    ref = amat.at[:, :, lanes((1 - c) * 128)]
    copy_to(ref, ref, a_send.at[1], a_recv.at[1 - c], partner).wait_recv()

    def c_pass(r, first=False):
        a = amat[:, :, r * 256 : r * 256 + 256].reshape(512, 256)
        res = jnp.dot(a, bmat[r * 256 : r * 256 + 256], preferred_element_type=F32)
        if first:
            cmat[...] = res.reshape(NZ, 64, COLS)
        else:
            cmat[...] += res.reshape(NZ, 64, COLS)

    g_start(2)
    for i in (0, 1):
        for r, h, to in ((3, i, 1), (1, 1 - i, 3)):
            b_arrived(r, c, h)
            if i == 0:
                b_start(b_copy(b_ref(r, c, h), 2, c, h, b_send.at[3, h], ydev(to)))
            b_start(b_copy(b_ref(r, c, h), r, c, h, b_send.at[4 if r == 3 else 5, h], partner))
    for h in (0, 1):
        b_arrived(0, 1 - c, h)
    c_pass(0, True)
    for h in (0, 1):
        b_arrived(2, c, h)
        b_start(b_copy(b_ref(2, c, h), 2, c, h, bp_send.at[h], partner))
    for r in (3, 1):
        for h in (0, 1):
            b_arrived(r, 1 - c, h)
        c_pass(r)
    for h in (0, 1):
        b_arrived(2, 1 - c, h)
    c_pass(2)

    z_sent = []
    for dist in (4, 3, 2, 1, 0):
        for p in (0, 1):
            for way in (0, 1):
                longest = 4 if p == way else 3
                if dist > longest:
                    continue
                zz = (z + NZ + (dist if way == 0 else -dist)) % NZ
                val = cmat[zz, :, p * 256 : p * 256 + 256]
                if dist < longest:
                    cp = copy_to(
                        zr.at[way, dist, p], zr.at[way, dist, p], z_send.at[way, dist, p], z_recv.at[way, dist, p], partner
                    )
                    cp.wait_recv()
                    val = val + zr[way, dist, p].astype(F32)
                if dist > 0:
                    zs[way, dist, p] = val.astype(BF16)
                    cp = copy_to(
                        zs.at[way, dist, p],
                        zr.at[way, dist - 1, p],
                        z_send.at[way, dist, p],
                        z_recv.at[way, dist - 1, p],
                        zdev(1 if way == 0 else -1),
                    )
                    cp.start()
                    z_sent.append(cp)
                elif way == 1:
                    total_p = val + zr[0, 0, p].astype(F32)
                    fx[yhi, :, p * 256 : p * 256 + 256] = total_p.astype(BF16)
        if dist in (4, 3):
            g_start(1 if dist == 4 else 3)
        if dist == 2:
            own = partial(0)
    fcp = copy_to(fx.at[yhi], fx.at[yhi], f_send, f_recv, other_box)
    fcp.start()

    for k in (1, 2, 3):
        copy_to(gr.at[k - 1], gr.at[k - 1], g_send.at[0], g_recv.at[k - 1], partner).wait_recv()
    summed = own + gr[0].astype(F32) + gr[1].astype(F32) + gr[2].astype(F32)
    gg_ref[...] = summed[:ROWS]
    cg_ref[...] = summed[ROWS : ROWS + 4]

    other = 1 - yhi
    copy_to(xb.at[other], xb.at[other], x_send, x_recv, other_box).wait_recv()
    xall = xb[...].reshape(16, COLS + 128)
    term = lax.dot_general(
        xall[:, COLS:].T.astype(BF16), xall[:, :COLS].astype(BF16), (((1,), (0,)), ((), ())), preferred_element_type=F32
    )
    bg_ref[...] = xall[4:5, :COLS] + xall[12:13, :COLS]
    copy_to(fx.at[other], fx.at[other], f_send, f_recv, other_box).wait_recv()
    wg_ref[...] = fx[...].astype(F32).reshape(128, COLS) + term

    for cp in sent + a_sent + b_sent + g_sent + z_sent + [xcp, fcp]:
        cp.wait_send()


def body(gens, center, weight, bias, phase, gens_cot, center_cot, offset_cot):
    vm = pl.BlockSpec(memory_space=pltpu.VMEM)
    hbm = pl.BlockSpec(memory_space=pl.ANY)
    dma = pltpu.SemaphoreType.DMA
    sds = jax.ShapeDtypeStruct
    outs = pl.pallas_call(
        kernel,
        out_shape=(
            sds((4, COLS), F32),
            sds((ROWS, COLS), BF16),
            sds((4, COLS), F32),
            sds((128, COLS), F32),
            sds((1, COLS), F32),
            sds((ROWS, 1024), F32),
            sds((4, 1024), F32),
        ),
        in_specs=[hbm, vm, hbm, vm, vm, vm, vm, vm],
        out_specs=(vm,) * 7,
        scratch_shapes=[
            pltpu.VMEM((D, COLS), BF16),
            pltpu.VMEM((WIDE, D), BF16),
            pltpu.VMEM((ROWS, COLS), F32),
            pltpu.VMEM((NZ, 8, COLS), F32),
            pltpu.VMEM((D, ROWS), BF16),
            pltpu.VMEM((NZ, 64, 1024), BF16),
            pltpu.VMEM((4, 8, COLS), F32),
            pltpu.VMEM((NZ, 8, COLS), F32),
            pltpu.VMEM((WIDE, COLS), BF16),
            pltpu.VMEM((1024, COLS), BF16),
            pltpu.VMEM((NZ, 64, COLS), F32),
            pltpu.VMEM((2, 5, 2, 64, 256), BF16),
            pltpu.VMEM((2, 5, 2, 64, 256), BF16),
            pltpu.VMEM((3, WIDE, 1024), BF16),
            pltpu.VMEM((3, WIDE, 1024), BF16),
            pltpu.VMEM((2, 64, COLS), BF16),
            pltpu.VMEM((2, 8, COLS + 128), F32),
            dma((3,)),
            dma((4, 64)),
            dma((64,)),
            dma((8,)),
            dma((8,)),
            dma((3,)),
            dma((3,)),
            dma((4,)),
            dma((4,)),
            dma((8,)),
            dma((8,)),
            dma((6, 2)),
            dma((16,)),
            dma((2,)),
            dma((3,)),
            dma((3,)),
            dma((2, 5, 2)),
            dma((2, 5, 2)),
            dma,
            dma,
            dma,
            dma,
        ],
        compiler_params=pltpu.CompilerParams(
            collective_id=0, has_side_effects=True, vmem_limit_bytes=56 * 1024 * 1024
        ),
        name="zonotope_step",
    )(
        gens.reshape(ROWS, D), center, weight, bias.reshape(1, COLS), phase,
        gens_cot.reshape(ROWS, COLS), center_cot, offset_cot,
    )
    center_out, gens_out, offset, weight_grad, bias_grad, gens_grad, center_grad = outs
    return (
        center_out, gens_out.reshape(4, 32, COLS), offset, weight_grad, bias_grad.reshape(COLS),
        gens_grad.reshape(4, 32, 1024), center_grad,
    )


def solution(mesh):
    return jax.shard_map(
        body,
        mesh=mesh,
        in_specs=(
            P("box", "gen", None),
            P("box", None),
            P("gen", "neur"),
            P("neur"),
            P("box", "neur"),
            P("box", "gen", "neur"),
            P("box", "neur"),
            P("box", "neur"),
        ),
        out_specs=(
            P("box", "neur"),
            P("box", "gen", "neur"),
            P("box", "neur"),
            P("gen", "neur"),
            P("neur"),
            P("box", "gen", "neur"),
            P("box", "neur"),
        ),
        check_vma=False,
    )
```

```python
import math

import jax
import jax.numpy as jnp
from jax import lax
from jax.experimental import pallas as pl
from jax.experimental.pallas import tpu as pltpu
from jax.sharding import PartitionSpec as P

MESH = pl.DeviceIdType.MESH
F32 = jnp.float32
BF16 = jnp.bfloat16

NZ = 8
D = 4096
COLS = 512
ROWS = 128
WIDE = 144
NH = 4
PIECE = 128 // NH
HALF = NH // 2
NP = 2
FP = COLS // NP


def neuron(center_pre, radius, phase):
    upper = center_pre + radius
    lower = center_pre - radius
    ratio = jnp.clip(upper / (upper - lower + 1e-05), 0.0, 1.0)
    active = (phase == 1).astype(center_pre.dtype)
    crossing = (phase == 2).astype(center_pre.dtype)
    slope = active + crossing * ratio
    offset = crossing * (-ratio * lower * 0.5)
    return (slope, slope * center_pre + offset, offset)


def zsteps(d):
    return {0: (0,), 4: (4,)}.get(d, (-d, d))


def kernel(
    gens_hbm, center_hbm, w_hbm, bias_hbm, phase_hbm, cot_hbm, ccot_hbm, ocot_hbm,
    cout_ref, gout_ref, off_ref, wg_ref, bg_ref, gg_ref, cg_ref,
    center_ref, bias_ref, phase_ref, cot_ref, ccot_ref, ocot_ref,
    w, wide, acc, cslot, gt, amat, sa, sb, bk, bmat, cmat, zs, zr, gs, gr, fx, xb,
    load_sem, out_sem, wz_sem, wy_sem, wp_sem, a_sem, s_sem, bo_sem, bf_sem, bp_sem, z_sem, f_sem, gx_sem,
):
    me = lax.axis_index("gen")
    x = lax.axis_index("neur")
    yhi = lax.axis_index("box")
    z = me // 4
    ylo = (me // 2) % 2
    c = me % 2
    y = yhi * 2 + ylo
    quad = ylo * 2 + c

    def dev(zz, yy, cc, xx=None):
        return (zz * 4 + (yy % 2) * 2 + cc, x if xx is None else xx, yy // 2)

    def zdev(k):
        return dev((z + NZ + k) % NZ, y, c)

    def ydev(k, cc=None):
        return dev(z, (y + k) % 4, c if cc is None else cc)

    def xdev(k):
        return dev(z, y, c, (x + k) % 4)

    partner = dev(z, y, 1 - c)
    other_box = ydev(2)

    sent = [0, 0, 0]

    def copy_to(src, dst, group, recv_sem, device):
        return pltpu.make_async_remote_copy(
            src_ref=src,
            dst_ref=dst,
            send_sem=out_sem.at[group],
            recv_sem=recv_sem,
            device_id=device,
            device_id_type=MESH,
        )

    def go(src, dst, group, recv_sem, device):
        copy_to(src, dst, group, recv_sem, device).start()
        sent[group] += math.prod(src.shape) * src.dtype.itemsize

    def await_bytes(ref, recv_sem):
        copy_to(ref, ref, 0, recv_sem, partner).wait_recv()

    barrier = pltpu.get_barrier_semaphore()
    peers = [partner, zdev(1), zdev(-1)] + [xdev(k) for k in (1, 2, 3)]
    peers += [ydev(k, cc) for k in (1, 2, 3) for cc in (0, 1)]
    for peer in peers:
        pl.semaphore_signal(barrier, inc=1, device_id=peer, device_id_type=MESH)

    loads = [
        pltpu.make_async_copy(src, dst, load_sem.at[i])
        for i, (src, dst) in enumerate(
            (
                (gens_hbm, wide.at[pl.ds(0, ROWS)]),
                (center_hbm, center_ref),
                (w_hbm, w.at[pl.ds(pl.multiple_of(me * 128, 128), 128)]),
                (bias_hbm, bias_ref),
                (phase_hbm, phase_ref),
                (cot_hbm, cot_ref),
                (ccot_hbm, ccot_ref),
                (ocot_hbm, ocot_ref),
            )
        )
    ]
    for cp in loads:
        cp.start()
    pl.semaphore_wait(barrier, len(peers))

    def chunk(zz, yl, cc, h=0, n=NH):
        at = (zz * 4 + yl * 2 + cc) * 128 + h * PIECE
        return w.at[pl.ds(pl.multiple_of(at, PIECE), n * PIECE)]

    def send_z(way, zz, h, own=False):
        ref = chunk(zz, ylo, c, h, 1)
        src = w_hbm.at[h * PIECE : h * PIECE + PIECE] if own else ref
        go(src, ref, 0, wz_sem.at[zz, h], zdev(1) if way == 0 else zdev(-1))

    def send_y(zz, h, n, own=False):
        ref = chunk(zz, ylo, c, h, n)
        src = w_hbm.at[h * PIECE : (h + n) * PIECE] if own else ref
        go(src, ref, 0, wy_sem.at[zz], ydev(1) if h < HALF else ydev(3))

    def send_p(zz, yl, own=False):
        ref = chunk(zz, yl, c)
        go(w_hbm if own else ref, ref, 0, wp_sem.at[zz], partner)

    for h in range(NH):
        send_z(0, z, h, own=True)
        send_z(1, z, NH - 1 - h, own=True)
    send_y(z, 0, HALF, own=True)
    send_y(z, HALF, HALF, own=True)
    send_p(z, ylo, own=True)

    loads[0].wait()

    def turn(i, carry):
        at = pl.multiple_of(i * 128, 128)
        gt[pl.ds(at, 128), :] = wide[0:ROWS, pl.ds(at, 128)].astype(F32).T.astype(BF16)
        return carry

    lax.fori_loop(8 * x, 8 * x + 8, turn, 0)
    gt3 = gt.reshape(NZ, 512, 128)

    def a_rows(yy, cc):
        return pl.ds(pl.multiple_of((yy % 2) * 256 + cc * 128 + (yy // 2) * 64, 64), 64)

    def lanes(at, n=128):
        return pl.ds(pl.multiple_of(at, 128), n)

    mine = pl.ds(2 * x, 2)
    for k in (2, 1, 3):
        r = 4 - k
        for cc in (0, 1):
            go(
                gt3.at[mine, a_rows((y + k) % 4, cc), :],
                amat.at[mine, :, lanes((r * 2 + c) * 128)],
                1,
                a_sem.at[0],
                ydev(k, cc),
            )

    loads[1].wait()
    wide[pl.ds(ROWS, 16)] = jnp.concatenate([center_ref[...].astype(F32), jnp.zeros((12, D), F32)], 0).astype(BF16)
    acc[...] = jnp.zeros_like(acc)
    lax.fori_loop(8 * x + 8, 8 * x + 32, lambda i, carry: turn(i % 32, carry), 0)
    own_a = pltpu.make_async_copy(gt3.at[:, a_rows(y, c), :], amat.at[:, :, lanes(c * 128)], load_sem.at[8])
    own_a.start()
    for cp in loads[2:]:
        cp.wait()

    def a_spread():
        ref = amat.at[mine, :, lanes(256, 768)]
        await_bytes(ref, a_sem.at[0])
        for k in (2, 1, 3):
            go(ref, ref, 1, a_sem.at[1], xdev(k))
        go(gt3.at[:, a_rows(y, 1 - c), :], amat.at[:, :, lanes(c * 128)], 1, a_sem.at[2], partner)

    def handle_y(d):
        for dz in zsteps(d):
            zz = (z + NZ + dz) % NZ
            await_bytes(chunk(zz, 1 - ylo, c), wy_sem.at[zz])
            send_p(zz, 1 - ylo)

    def compute(d):
        for dz in zsteps(d):
            zz = (z + NZ + dz) % NZ
            await_bytes(chunk(zz, 0, 0, 0, 2 * NH), wp_sem.at[zz])
            at = pl.ds(pl.multiple_of(zz * 512, 512), 512)
            res = jnp.dot(wide[:, at], w[at, :], preferred_element_type=F32)
            acc[...] += res[:ROWS]
            cslot[zz] = res[ROWS : ROWS + 8]

    for d in (1, 2, 3, 4):
        for i in range(NH):
            for way in (0, 1):
                h = i if way == 0 else NH - 1 - i
                if d == 4 and i >= HALF:
                    continue
                zz = (z + NZ - d) % NZ if way == 0 else (z + d) % NZ
                await_bytes(chunk(zz, ylo, c, h, 1), wz_sem.at[zz, h])
                if d < 3 or (d == 3 and i < HALF):
                    send_z(way, zz, h)
                if d == 4:
                    send_y(zz, h, 1)
                elif i % HALF == HALF - 1:
                    send_y(zz, 0 if h < HALF else HALF, HALF)
        for dz in zsteps(d):
            send_p((z + NZ + dz) % NZ, ylo)
        if d >= 2:
            handle_y(d - 2)
        if d == 2:
            a_spread()
        if d >= 3:
            compute(d - 3)
    handle_y(3)
    compute(2)
    handle_y(4)
    compute(3)
    compute(4)

    gen_pre = acc[...]
    cot = cot_ref[...].astype(F32)
    part_radius = jnp.sum(jnp.abs(gen_pre).reshape(4, 32, COLS), axis=1)
    part_inner = jnp.sum((cot * gen_pre).reshape(4, 32, COLS), axis=1)
    sa[quad] = jnp.concatenate([part_radius, part_inner], 0)
    for k in (1, 2, 3):
        go(sa.at[quad], sa.at[quad], 1, s_sem.at[0], (z * 4 + (quad + k) % 4, x, yhi))
    await_bytes(sa.at[pl.ds(0, 3)], s_sem.at[0])
    sb[z] = (sa[0] + sa[1]) + (sa[2] + sa[3])
    for k in (4, 3, 5, 2, 6, 1, 7):
        go(sb.at[z], sb.at[z], 1, s_sem.at[1], zdev(k))
    center_pre = cslot[0][0:4]
    for i in range(1, NZ):
        center_pre = center_pre + cslot[i][0:4]
    center_pre = center_pre + bias_ref[...]
    await_bytes(sb.at[pl.ds(0, NZ - 1)], s_sem.at[1])
    total = ((sb[0] + sb[1]) + (sb[2] + sb[3])) + ((sb[4] + sb[5]) + (sb[6] + sb[7]))
    radius = total[0:4]
    intersection = total[4:8]

    phase = phase_ref[...]
    (slope, center_out, offset), pull = jax.vjp(lambda a, b: neuron(a, b, phase), center_pre, radius)
    g_center, g_radius = pull((intersection, ccot_ref[...], ocot_ref[...]))
    pre3 = gen_pre.reshape(4, 32, COLS)
    sign = jnp.where(pre3 > 0, 1.0, jnp.where(pre3 < 0, -1.0, 0.0))
    back = (slope[:, None, :] * cot.reshape(4, 32, COLS) + sign * g_radius[:, None, :]).astype(BF16).reshape(ROWS, COLS)
    bk[0:ROWS] = back
    bmat[pl.ds(pl.multiple_of(c * 128, 128), 128)] = back

    def b_part(r, cc, p, i=0, n=64):
        return bmat.at[pl.ds(pl.multiple_of((r * 2 + cc) * 128 + i * 64, 64), n), pl.ds(p * FP, FP)]

    def bk_part(p, i=0, n=64):
        return bk.at[i * 64 : i * 64 + n, pl.ds(p * FP, FP)]

    for p in range(NP):
        for i in (0, 1):
            j = 1 - i
            go(bk_part(p, i), b_part(3, c, p, i), 2, bo_sem.at[0, i, p], ydev(1))
            go(bk_part(p, j), b_part(1, c, p, j), 2, bo_sem.at[1, j, p], ydev(3))
        go(bk_part(p, 0, 128), b_part(0, c, p, 0, 128), 2, bp_sem.at[0, p], partner)

    center_back = g_center.astype(BF16).astype(F32)
    bk[pl.ds(ROWS, 16)] = jnp.concatenate([center_back, jnp.zeros((12, COLS), F32)], 0).astype(BF16)
    xb[yhi, :, 0:COLS] = jnp.concatenate([center_back, jnp.sum(g_center, axis=0, keepdims=True), jnp.zeros((3, COLS), F32)], 0)
    xb[yhi, :, COLS:] = jnp.concatenate(
        [
            jnp.concatenate([center_ref[:, lanes(me * 128)].astype(F32), jnp.zeros((4, 128), F32)], 0),
            jnp.zeros((8, COLS - 128), F32),
        ],
        1,
    )
    go(xb.at[yhi], xb.at[yhi], 2, gx_sem.at[1], other_box)

    def partial(k):
        at = pl.ds(pl.multiple_of(((x + k) % 4) * 1024, 1024), 1024)
        return lax.dot_general(bk[...], w[at, :], (((1,), (1,)), ((), ())), preferred_element_type=F32)

    for k in (2, 1, 3):
        gs[k - 1] = partial(k).astype(BF16)
        go(gs.at[k - 1], gr.at[3 - k], 2, gx_sem.at[0], xdev(k))

    cout_ref[...] = center_out
    off_ref[...] = offset
    gout_ref[...] = (slope[:, None, :] * pre3).astype(BF16).reshape(ROWS, COLS)

    own_a.wait()
    spread = gt.at[pl.ds(0, 3 * 2 * 64 * 6)]
    await_bytes(spread, a_sem.at[1])
    await_bytes(amat.at[:, :, lanes((1 - c) * 128)], a_sem.at[2])

    def b_forward(p):
        for i in (0, 1):
            for r, h, to in ((3, i, 1), (1, 1 - i, 3)):
                await_bytes(b_part(r, c, p, h), bo_sem.at[0 if r == 3 else 1, h, p])
                if i == 0:
                    go(b_part(r, c, p, h), b_part(2, c, p, h), 2, bf_sem.at[p], ydev(to))
        for r in (3, 1):
            go(b_part(r, c, p, 0, 128), b_part(r, c, p, 0, 128), 2, bp_sem.at[r, p], partner)

    def b_last(p):
        ref = b_part(2, c, p, 0, 128)
        await_bytes(ref, bf_sem.at[p])
        go(ref, ref, 2, bp_sem.at[2, p], partner)

    def c_pass(r, p):
        await_bytes(b_part(r, 1 - c, p, 0, 128), bp_sem.at[r, p])
        a = amat[:, :, r * 256 : r * 256 + 256].reshape(512, 256)
        cols = pl.ds(p * FP, FP)
        res = jnp.dot(a, bmat[r * 256 : r * 256 + 256, cols], preferred_element_type=F32).reshape(NZ, 64, FP)
        if r == 0:
            cmat[:, :, cols] = res
        else:
            cmat[:, :, cols] += res

    def z_step(dist, p):
        for way in (0, 1):
            longest = 4 if p % 2 == way else 3
            if dist > longest:
                continue
            val = cmat[(z + NZ + (dist if way == 0 else -dist)) % NZ, :, pl.ds(p * FP, FP)]
            if dist < longest:
                await_bytes(zr.at[way, dist, p], z_sem.at[way, dist, p])
                val = val + zr[way, dist, p].astype(F32)
            if dist > 0:
                zs[way, dist, p] = val.astype(BF16)
                to = zdev(1 if way == 0 else -1)
                go(zs.at[way, dist, p], zr.at[way, dist - 1, p], 2, z_sem.at[way, dist - 1, p], to)
            elif way == 1:
                val = val + zr[0, 0, p].astype(F32)
                fx[yhi, p] = val.astype(BF16)
                go(fx.at[yhi, p], fx.at[yhi, p], 2, f_sem.at[p], other_box)

    for p in range(NP):
        b_forward(p)
    for p in range(NP):
        for r in (0, 3, 1):
            c_pass(r, p)
        b_last(p)
        c_pass(2, p)
        z_step(4, p)
        if p > 0:
            z_step(3, p - 1)
    z_step(3, NP - 1)
    own = partial(0)
    for dist in (2, 1, 0):
        for p in range(NP):
            z_step(dist, p)

    await_bytes(gr, gx_sem.at[0])
    summed = own + gr[0].astype(F32) + gr[1].astype(F32) + gr[2].astype(F32)
    gg_ref[...] = summed[:ROWS]
    cg_ref[...] = summed[ROWS : ROWS + 4]

    other = 1 - yhi
    await_bytes(xb.at[other], gx_sem.at[1])
    xall = xb[:, :, 0 : COLS + 128].reshape(16, COLS + 128)
    term = lax.dot_general(
        xall[:, COLS:].T.astype(BF16), xall[:, :COLS].astype(BF16), (((1,), (0,)), ((), ())), preferred_element_type=F32
    )
    bg_ref[...] = xall[4:5, :COLS] + xall[12:13, :COLS]
    for p in range(NP):
        await_bytes(fx.at[other, p], f_sem.at[p])
        at = p * FP
        wg_ref[:, at : at + FP] = fx[:, p].astype(F32).reshape(128, FP) + term[:, at : at + FP]

    for group, count in enumerate(sent):
        ref = w.at[pl.ds(0, count // (COLS * 2))]
        copy_to(ref, ref, group, out_sem.at[group], partner).wait_send()


def finish(*refs):
    for src, dst in zip(refs[:7], refs[7:]):
        dst[...] = src[...]


def body(gens, center, weight, bias, phase, gens_cot, center_cot, offset_cot):
    vm = pl.BlockSpec(memory_space=pltpu.VMEM)
    hbm = pl.BlockSpec(memory_space=pltpu.HBM)
    dma = pltpu.SemaphoreType.DMA
    sds = jax.ShapeDtypeStruct
    outs = pl.pallas_call(
        kernel,
        out_shape=(
            sds((4, COLS), F32),
            sds((ROWS, COLS), BF16),
            sds((4, COLS), F32),
            sds((128, COLS), F32),
            sds((1, COLS), F32),
            sds((ROWS, 1024), F32),
            sds((4, 1024), F32),
        ),
        in_specs=[hbm] * 8,
        out_specs=(vm,) * 7,
        scratch_shapes=[
            pltpu.VMEM((4, D), BF16),
            pltpu.VMEM((1, COLS), F32),
            pltpu.VMEM((4, COLS), jnp.int32),
            pltpu.VMEM((ROWS, COLS), BF16),
            pltpu.VMEM((4, COLS), F32),
            pltpu.VMEM((4, COLS), F32),
            pltpu.VMEM((D, COLS), BF16),
            pltpu.VMEM((WIDE, D), BF16),
            pltpu.VMEM((ROWS, COLS), F32),
            pltpu.VMEM((NZ, 8, COLS), F32),
            pltpu.VMEM((D, ROWS), BF16),
            pltpu.VMEM((NZ, 64, 1024), BF16),
            pltpu.VMEM((4, 8, COLS), F32),
            pltpu.VMEM((NZ, 8, COLS), F32),
            pltpu.VMEM((WIDE, COLS), BF16),
            pltpu.VMEM((1024, COLS), BF16),
            pltpu.VMEM((NZ, 64, COLS), F32),
            pltpu.VMEM((2, 5, NP, 64, FP), BF16),
            pltpu.VMEM((2, 5, NP, 64, FP), BF16),
            pltpu.VMEM((3, WIDE, 1024), BF16),
            pltpu.VMEM((3, WIDE, 1024), BF16),
            pltpu.VMEM((2, NP, 64, FP), BF16),
            pltpu.VMEM((2, 8, 2 * COLS), F32),
            dma((9,)),
            dma((3,)),
            dma((NZ, NH)),
            dma((NZ,)),
            dma((NZ,)),
            dma((3,)),
            dma((2,)),
            dma((2, 2, NP)),
            dma((NP,)),
            dma((4, NP)),
            dma((2, 4, NP)),
            dma((NP,)),
            dma((2,)),
        ],
        compiler_params=pltpu.CompilerParams(
            collective_id=0, has_side_effects=True, vmem_limit_bytes=32 * 1024 * 1024
        ),
        name="zonotope_step",
    )(
        *(
            pltpu.with_memory_space_constraint(v, pltpu.HBM)
            for v in (
                gens.reshape(ROWS, D), center, weight, bias.reshape(1, COLS), phase,
                gens_cot.reshape(ROWS, COLS), center_cot, offset_cot,
            )
        )
    )
    outs = pl.pallas_call(
        finish,
        out_shape=tuple(sds(o.shape, o.dtype) for o in outs),
        in_specs=[vm] * 7,
        out_specs=(vm,) * 7,
        compiler_params=pltpu.CompilerParams(vmem_limit_bytes=8 * 1024 * 1024),
        name="finish",
    )(*outs)
    center_out, gens_out, offset, weight_grad, bias_grad, gens_grad, center_grad = outs
    return (
        center_out, gens_out.reshape(4, 32, COLS), offset, weight_grad, bias_grad.reshape(COLS),
        gens_grad.reshape(4, 32, 1024), center_grad,
    )


def solution(mesh):
    return jax.shard_map(
        body,
        mesh=mesh,
        in_specs=(
            P("box", "gen", None),
            P("box", None),
            P("gen", "neur"),
            P("neur"),
            P("box", "neur"),
            P("box", "gen", "neur"),
            P("box", "neur"),
            P("box", "neur"),
        ),
        out_specs=(
            P("box", "neur"),
            P("box", "gen", "neur"),
            P("box", "neur"),
            P("gen", "neur"),
            P("neur"),
            P("box", "gen", "neur"),
            P("box", "neur"),
        ),
        check_vma=False,
    )
```

```python
import math

import jax
import jax.numpy as jnp
from jax import lax
from jax.experimental import pallas as pl
from jax.experimental.pallas import tpu as pltpu
from jax.sharding import PartitionSpec as P

MESH = pl.DeviceIdType.MESH
F32 = jnp.float32
BF16 = jnp.bfloat16

NZ = 8
D = 4096
COLS = 512
ROWS = 128
WIDE = 144
NH = 4
PIECE = 128 // NH
HALF = NH // 2
NQ = 2
FQ = COLS // NQ


def neuron(center_pre, radius, phase):
    upper = center_pre + radius
    lower = center_pre - radius
    ratio = jnp.clip(upper / (upper - lower + 1e-05), 0.0, 1.0)
    active = (phase == 1).astype(center_pre.dtype)
    crossing = (phase == 2).astype(center_pre.dtype)
    slope = active + crossing * ratio
    offset = crossing * (-ratio * lower * 0.5)
    return (slope, slope * center_pre + offset, offset)


def zsteps(d):
    return {0: (0,), 4: (4,)}.get(d, (-d, d))


def kernel(
    gens_hbm, center_hbm, w_hbm, bias_hbm, phase_hbm, cot_hbm, ccot_hbm, ocot_hbm,
    cout_ref, gout_ref, off_ref, wg_ref, bg_ref, gg_ref, cg_ref,
    center_ref, bias_ref, phase_ref, ccot_ref, ocot_ref,
    w, wide, acc, cslot, gt, amat, sa, sb, bk, call, sall, xs, cmat, zs, zr, gs, gr, fx, xb,
    load_sem, out_sem, wz_sem, wy_sem, wp_sem, a_sem, s_sem, near_sem, far_sem, pair_sem, f_sem, gx_sem,
):
    me = lax.axis_index("gen")
    x = lax.axis_index("neur")
    yhi = lax.axis_index("box")
    z = me // 4
    ylo = (me // 2) % 2
    c = me % 2
    y = yhi * 2 + ylo
    quad = ylo * 2 + c

    def dev(zz, yy, cc, xx=None):
        return (zz * 4 + (yy % 2) * 2 + cc, x if xx is None else xx, yy // 2)

    def zdev(k):
        return dev((z + NZ + k) % NZ, y, c)

    def ydev(k, cc=None):
        return dev(z, (y + k) % 4, c if cc is None else cc)

    def xdev(k):
        return dev(z, y, c, (x + k) % 4)

    partner = dev(z, y, 1 - c)
    other_box = ydev(2)

    sent = [0, 0, 0]

    def copy_to(src, dst, group, recv_sem, device):
        return pltpu.make_async_remote_copy(
            src_ref=src,
            dst_ref=dst,
            send_sem=out_sem.at[group],
            recv_sem=recv_sem,
            device_id=device,
            device_id_type=MESH,
        )

    def go(src, dst, group, recv_sem, device):
        copy_to(src, dst, group, recv_sem, device).start()
        sent[group] += math.prod(src.shape) * src.dtype.itemsize

    def await_bytes(ref, recv_sem):
        copy_to(ref, ref, 0, recv_sem, partner).wait_recv()

    barrier = pltpu.get_barrier_semaphore()
    peers = [partner, zdev(1), zdev(-1)] + [xdev(k) for k in (1, 2, 3)]
    peers += [ydev(k, cc) for k in (1, 2, 3) for cc in (0, 1)]
    for peer in peers:
        pl.semaphore_signal(barrier, inc=1, device_id=peer, device_id_type=MESH)

    loads = [
        pltpu.make_async_copy(src, dst, load_sem.at[i])
        for i, (src, dst) in enumerate(
            (
                (gens_hbm, wide.at[pl.ds(0, ROWS)]),
                (center_hbm, center_ref),
                (w_hbm, w.at[pl.ds(pl.multiple_of(me * 128, 128), 128)]),
                (bias_hbm, bias_ref),
                (phase_hbm, phase_ref),
                (cot_hbm, call.at[pl.ds(pl.multiple_of(c * 128, 128), 128)]),
                (ccot_hbm, ccot_ref),
                (ocot_hbm, ocot_ref),
            )
        )
    ]
    for cp in loads:
        cp.start()
    pl.semaphore_wait(barrier, len(peers))

    def chunk(zz, yl, cc, h=0, n=NH):
        at = (zz * 4 + yl * 2 + cc) * 128 + h * PIECE
        return w.at[pl.ds(pl.multiple_of(at, PIECE), n * PIECE)]

    def send_z(way, zz, h, own=False):
        ref = chunk(zz, ylo, c, h, 1)
        src = w_hbm.at[h * PIECE : h * PIECE + PIECE] if own else ref
        go(src, ref, 0, wz_sem.at[zz, h], zdev(1) if way == 0 else zdev(-1))

    def send_y(zz, h, n, own=False):
        ref = chunk(zz, ylo, c, h, n)
        src = w_hbm.at[h * PIECE : (h + n) * PIECE] if own else ref
        go(src, ref, 0, wy_sem.at[zz], ydev(1) if h < HALF else ydev(3))

    def send_p(zz, yl, own=False):
        ref = chunk(zz, yl, c)
        go(w_hbm if own else ref, ref, 0, wp_sem.at[zz], partner)

    for h in range(NH):
        send_z(0, z, h, own=True)
        send_z(1, z, NH - 1 - h, own=True)
    send_y(z, 0, HALF, own=True)
    send_y(z, HALF, HALF, own=True)
    send_p(z, ylo, own=True)

    loads[0].wait()

    def turn(i, carry):
        at = pl.multiple_of(i * 128, 128)
        gt[pl.ds(at, 128), :] = wide[0:ROWS, pl.ds(at, 128)].astype(F32).T.astype(BF16)
        return carry

    lax.fori_loop(8 * x, 8 * x + 8, turn, 0)
    gt3 = gt.reshape(NZ, 512, 128)

    def a_rows(yy, cc):
        return pl.ds(pl.multiple_of((yy % 2) * 256 + cc * 128 + (yy // 2) * 64, 64), 64)

    def lanes(at, n=128):
        return pl.ds(pl.multiple_of(at, 128), n)

    mine = pl.ds(2 * x, 2)
    for k in (2, 1, 3):
        r = 4 - k
        for cc in (0, 1):
            go(
                gt3.at[mine, a_rows((y + k) % 4, cc), :],
                amat.at[mine, :, lanes((r * 2 + c) * 128)],
                1,
                a_sem.at[0],
                ydev(k, cc),
            )

    loads[1].wait()
    wide[pl.ds(ROWS, 16)] = jnp.concatenate([center_ref[...].astype(F32), jnp.zeros((12, D), F32)], 0).astype(BF16)
    acc[...] = jnp.zeros_like(acc)
    lax.fori_loop(8 * x + 8, 8 * x + 32, lambda i, carry: turn(i % 32, carry), 0)
    own_a = pltpu.make_async_copy(gt3.at[:, a_rows(y, c), :], amat.at[:, :, lanes(c * 128)], load_sem.at[8])
    own_a.start()
    for cp in loads[2:]:
        cp.wait()

    def a_spread():
        ref = amat.at[mine, :, lanes(256, 768)]
        await_bytes(ref, a_sem.at[0])
        for k in (2, 1, 3):
            go(ref, ref, 1, a_sem.at[1], xdev(k))
        go(gt3.at[:, a_rows(y, 1 - c), :], amat.at[:, :, lanes(c * 128)], 1, a_sem.at[2], partner)

    def handle_y(d):
        for dz in zsteps(d):
            zz = (z + NZ + dz) % NZ
            await_bytes(chunk(zz, 1 - ylo, c), wy_sem.at[zz])
            send_p(zz, 1 - ylo)

    def compute(d):
        for dz in zsteps(d):
            zz = (z + NZ + dz) % NZ
            await_bytes(chunk(zz, 0, 0, 0, 2 * NH), wp_sem.at[zz])
            at = pl.ds(pl.multiple_of(zz * 512, 512), 512)
            res = jnp.dot(wide[:, at], w[at, :], preferred_element_type=F32)
            acc[...] += res[:ROWS]
            cslot[zz] = res[ROWS : ROWS + 8]

    held = (call, sall)

    def part(b, r, cc, i=0, n=64):
        return held[b].at[pl.ds(pl.multiple_of((r * 2 + cc) * 128 + i * 64, 64), n)]

    def gather_own(b):
        for i in (0, 1):
            j = 1 - i
            go(part(b, 0, c, i), part(b, 3, c, i), 2, near_sem.at[b, i], ydev(1))
            go(part(b, 0, c, j), part(b, 1, c, j), 2, near_sem.at[b, 2 + j], ydev(3))
        go(part(b, 0, c, 0, 128), part(b, 0, c, 0, 128), 2, pair_sem.at[b, 0], partner)

    def gather_forward(b):
        for i in (0, 1):
            for r, h, to in ((3, i, 1), (1, 1 - i, 3)):
                await_bytes(part(b, r, c, h), near_sem.at[b, h if r == 3 else 2 + h])
                if i == 0:
                    go(part(b, r, c, h), part(b, 2, c, h), 2, far_sem.at[b], ydev(to))
        for r in (3, 1):
            go(part(b, r, c, 0, 128), part(b, r, c, 0, 128), 2, pair_sem.at[b, r], partner)

    def gather_last(b):
        ref = part(b, 2, c, 0, 128)
        await_bytes(ref, far_sem.at[b])
        go(ref, ref, 2, pair_sem.at[b, 2], partner)

    for d in (1, 2, 3, 4):
        for i in range(NH):
            for way in (0, 1):
                h = i if way == 0 else NH - 1 - i
                if d == 4 and i >= HALF:
                    continue
                zz = (z + NZ - d) % NZ if way == 0 else (z + d) % NZ
                await_bytes(chunk(zz, ylo, c, h, 1), wz_sem.at[zz, h])
                if d < 3 or (d == 3 and i < HALF):
                    send_z(way, zz, h)
                if d == 4:
                    send_y(zz, h, 1)
                elif i % HALF == HALF - 1:
                    send_y(zz, 0 if h < HALF else HALF, HALF)
        for dz in zsteps(d):
            send_p((z + NZ + dz) % NZ, ylo)
        if d == 4:
            gather_own(0)
        if d >= 2:
            handle_y(d - 2)
        if d == 2:
            a_spread()
        if d >= 3:
            compute(d - 3)
    handle_y(3)
    compute(2)
    handle_y(4)
    compute(3)
    compute(4)

    gen_pre = acc[...]
    cot = call[pl.ds(pl.multiple_of(c * 128, 128), 128)].astype(F32)
    part_radius = jnp.sum(jnp.abs(gen_pre).reshape(4, 32, COLS), axis=1)
    part_inner = jnp.sum((cot * gen_pre).reshape(4, 32, COLS), axis=1)
    sa[quad] = jnp.concatenate([part_radius, part_inner], 0)
    for k in (1, 2, 3):
        go(sa.at[quad], sa.at[quad], 1, s_sem.at[0], (z * 4 + (quad + k) % 4, x, yhi))
    pre3 = gen_pre.reshape(4, 32, COLS)
    sign = jnp.where(pre3 > 0, 1.0, jnp.where(pre3 < 0, -1.0, 0.0))
    sall[pl.ds(pl.multiple_of(c * 128, 128), 128)] = sign.reshape(ROWS, COLS).astype(BF16)
    gather_own(1)
    await_bytes(sa.at[pl.ds(0, 3)], s_sem.at[0])
    sb[z] = (sa[0] + sa[1]) + (sa[2] + sa[3])
    for k in (4, 3, 5, 2, 6, 1, 7):
        go(sb.at[z], sb.at[z], 1, s_sem.at[1], zdev(k))
    center_pre = cslot[0][0:4]
    for i in range(1, NZ):
        center_pre = center_pre + cslot[i][0:4]
    center_pre = center_pre + bias_ref[...]
    gather_forward(0)
    gather_forward(1)
    gather_last(0)
    await_bytes(sb.at[pl.ds(0, NZ - 1)], s_sem.at[1])
    total = ((sb[0] + sb[1]) + (sb[2] + sb[3])) + ((sb[4] + sb[5]) + (sb[6] + sb[7]))
    radius = total[0:4]
    intersection = total[4:8]

    phase = phase_ref[...]
    (slope, center_out, offset), pull = jax.vjp(lambda a, b: neuron(a, b, phase), center_pre, radius)
    g_center, g_radius = pull((intersection, ccot_ref[...], ocot_ref[...]))
    back = (slope[:, None, :] * cot.reshape(4, 32, COLS) + sign * g_radius[:, None, :]).astype(BF16).reshape(ROWS, COLS)
    bk[0:ROWS] = back
    xs[yhi] = jnp.concatenate([slope, g_radius], 0)
    go(xs.at[yhi], xs.at[yhi], 2, gx_sem.at[2], ydev(3 - 2 * ylo))

    center_back = g_center.astype(BF16).astype(F32)
    bk[pl.ds(ROWS, 16)] = jnp.concatenate([center_back, jnp.zeros((12, COLS), F32)], 0).astype(BF16)
    xb[yhi, :, 0:COLS] = jnp.concatenate([center_back, jnp.sum(g_center, axis=0, keepdims=True), jnp.zeros((3, COLS), F32)], 0)
    xb[yhi, :, COLS:] = jnp.concatenate(
        [
            jnp.concatenate([center_ref[:, lanes(me * 128)].astype(F32), jnp.zeros((4, 128), F32)], 0),
            jnp.zeros((8, COLS - 128), F32),
        ],
        1,
    )
    go(xb.at[yhi], xb.at[yhi], 2, gx_sem.at[1], other_box)

    def partial(k):
        at = pl.ds(pl.multiple_of(((x + k) % 4) * 1024, 1024), 1024)
        return lax.dot_general(bk[...], w[at, :], (((1,), (1,)), ((), ())), preferred_element_type=F32)

    def g_start(k):
        gs[k - 1] = partial(k).astype(BF16)
        go(gs.at[k - 1], gr.at[3 - k], 2, gx_sem.at[0], xdev(k))

    def have(r):
        for b in (0, 1):
            await_bytes(part(b, r, 1 - c, 0, 128), pair_sem.at[b, r])

    def c_pass(r, box, at, n, first=False):
        cols = pl.ds(at, n)
        rows = pl.ds(pl.multiple_of(r * 256, 256), 256)
        scale = xs[box, 0:4, cols][None, :, None, :]
        g_rad = xs[box, 4:8, cols][None, :, None, :]
        cots = call[rows, cols].astype(F32).reshape(2, 4, 32, n)
        signs = sall[rows, cols].astype(F32).reshape(2, 4, 32, n)
        back = (scale * cots + signs * g_rad).astype(BF16).reshape(256, n)
        a = amat[:, :, lanes(r * 256, 256)].reshape(512, 256)
        res = jnp.dot(a, back, preferred_element_type=F32).reshape(NZ, 64, n)
        if first:
            cmat[:, :, cols] = res
        else:
            cmat[:, :, cols] += res

    g_start(2)
    own_a.wait()
    await_bytes(gt.at[pl.ds(0, 3 * 2 * 64 * 6)], a_sem.at[1])
    await_bytes(amat.at[:, :, lanes((1 - c) * 128)], a_sem.at[2])
    gather_last(1)
    have(0)
    c_pass(0, yhi, 0, COLS, first=True)
    g_start(1)
    have(3)
    have(1)
    c_pass(1 + 2 * ylo, yhi, 0, COLS)
    g_start(3)
    cout_ref[...] = center_out
    off_ref[...] = offset
    gout_ref[...] = (slope[:, None, :] * pre3).astype(BF16).reshape(ROWS, COLS)
    await_bytes(xs.at[1 - yhi], gx_sem.at[2])
    c_pass(3 - 2 * ylo, 1 - yhi, 0, COLS)
    have(2)

    def z_step(dist, q):
        for way in (0, 1):
            longest = 4 if q % 2 == way else 3
            if dist > longest:
                continue
            val = cmat[(z + NZ + (dist if way == 0 else -dist)) % NZ, :, pl.ds(q * FQ, FQ)]
            if dist < longest:
                await_bytes(zr.at[way, dist, q], wz_sem.at[way * 4 + dist, q])
                val = val + zr[way, dist, q].astype(F32)
            if dist > 0:
                zs[way, dist, q] = val.astype(BF16)
                to = zdev(1 if way == 0 else -1)
                go(zs.at[way, dist, q], zr.at[way, dist - 1, q], 2, wz_sem.at[way * 4 + dist - 1, q], to)
            elif way == 1:
                val = val + zr[0, 0, q].astype(F32)
                fx[yhi, q] = val.astype(BF16)
                go(fx.at[yhi, q], fx.at[yhi, q], 2, f_sem.at[q], other_box)

    for q in range(NQ):
        c_pass(2, 1 - yhi, q * FQ, FQ)
        z_step(4, q)
    for q in range(NQ):
        z_step(3, q)
    own = partial(0)
    for dist in (2, 1, 0):
        for q in range(NQ):
            z_step(dist, q)

    await_bytes(gr, gx_sem.at[0])
    summed = own + gr[0].astype(F32) + gr[1].astype(F32) + gr[2].astype(F32)
    gg_ref[...] = summed[:ROWS]
    cg_ref[...] = summed[ROWS : ROWS + 4]

    other = 1 - yhi
    await_bytes(xb.at[other], gx_sem.at[1])
    xall = xb[:, :, 0 : COLS + 128].reshape(16, COLS + 128)
    term = lax.dot_general(
        xall[:, COLS:].T.astype(BF16), xall[:, :COLS].astype(BF16), (((1,), (0,)), ((), ())), preferred_element_type=F32
    )
    bg_ref[...] = xall[4:5, :COLS] + xall[12:13, :COLS]
    for q in range(NQ):
        await_bytes(fx.at[other, q], f_sem.at[q])
        at = q * FQ
        wg_ref[:, at : at + FQ] = fx[:, q].astype(F32).reshape(128, FQ) + term[:, at : at + FQ]

    for group, count in enumerate(sent):
        ref = w.at[pl.ds(0, count // (COLS * 2))]
        copy_to(ref, ref, group, out_sem.at[group], partner).wait_send()


def finish(*refs):
    for src, dst in zip(refs[:7], refs[7:]):
        dst[...] = src[...]


def body(gens, center, weight, bias, phase, gens_cot, center_cot, offset_cot):
    vm = pl.BlockSpec(memory_space=pltpu.VMEM)
    hbm = pl.BlockSpec(memory_space=pltpu.HBM)
    dma = pltpu.SemaphoreType.DMA
    sds = jax.ShapeDtypeStruct
    outs = pl.pallas_call(
        kernel,
        out_shape=(
            sds((4, COLS), F32),
            sds((ROWS, COLS), BF16),
            sds((4, COLS), F32),
            sds((128, COLS), F32),
            sds((1, COLS), F32),
            sds((ROWS, 1024), F32),
            sds((4, 1024), F32),
        ),
        in_specs=[hbm] * 8,
        out_specs=(vm,) * 7,
        scratch_shapes=[
            pltpu.VMEM((4, D), BF16),
            pltpu.VMEM((1, COLS), F32),
            pltpu.VMEM((4, COLS), jnp.int32),
            pltpu.VMEM((4, COLS), F32),
            pltpu.VMEM((4, COLS), F32),
            pltpu.VMEM((D, COLS), BF16),
            pltpu.VMEM((WIDE, D), BF16),
            pltpu.VMEM((ROWS, COLS), F32),
            pltpu.VMEM((NZ, 8, COLS), F32),
            pltpu.VMEM((D, ROWS), BF16),
            pltpu.VMEM((NZ, 64, 1024), BF16),
            pltpu.VMEM((4, 8, COLS), F32),
            pltpu.VMEM((NZ, 8, COLS), F32),
            pltpu.VMEM((WIDE, COLS), BF16),
            pltpu.VMEM((1024, COLS), BF16),
            pltpu.VMEM((1024, COLS), BF16),
            pltpu.VMEM((2, 8, COLS), F32),
            pltpu.VMEM((NZ, 64, COLS), F32),
            pltpu.VMEM((2, 5, NQ, 64, FQ), BF16),
            pltpu.VMEM((2, 5, NQ, 64, FQ), BF16),
            pltpu.VMEM((3, WIDE, 1024), BF16),
            pltpu.VMEM((3, WIDE, 1024), BF16),
            pltpu.VMEM((2, NQ, 64, FQ), BF16),
            pltpu.VMEM((2, 8, 2 * COLS), F32),
            dma((9,)),
            dma((3,)),
            dma((NZ, NH)),
            dma((NZ,)),
            dma((NZ,)),
            dma((3,)),
            dma((2,)),
            dma((2, 4)),
            dma((2,)),
            dma((2, 4)),
            dma((NQ,)),
            dma((3,)),
        ],
        compiler_params=pltpu.CompilerParams(
            collective_id=0, has_side_effects=True, vmem_limit_bytes=32 * 1024 * 1024
        ),
        name="zonotope_step",
    )(
        *(
            pltpu.with_memory_space_constraint(v, pltpu.HBM)
            for v in (
                gens.reshape(ROWS, D), center, weight, bias.reshape(1, COLS), phase,
                gens_cot.reshape(ROWS, COLS), center_cot, offset_cot,
            )
        )
    )
    outs = pl.pallas_call(
        finish,
        out_shape=tuple(sds(o.shape, o.dtype) for o in outs),
        in_specs=[vm] * 7,
        out_specs=(vm,) * 7,
        compiler_params=pltpu.CompilerParams(vmem_limit_bytes=8 * 1024 * 1024),
        name="finish",
    )(*outs)
    center_out, gens_out, offset, weight_grad, bias_grad, gens_grad, center_grad = outs
    return (
        center_out, gens_out.reshape(4, 32, COLS), offset, weight_grad, bias_grad.reshape(COLS),
        gens_grad.reshape(4, 32, 1024), center_grad,
    )


def solution(mesh):
    return jax.shard_map(
        body,
        mesh=mesh,
        in_specs=(
            P("box", "gen", None),
            P("box", None),
            P("gen", "neur"),
            P("neur"),
            P("box", "neur"),
            P("box", "gen", "neur"),
            P("box", "neur"),
            P("box", "neur"),
        ),
        out_specs=(
            P("box", "neur"),
            P("box", "gen", "neur"),
            P("box", "neur"),
            P("gen", "neur"),
            P("neur"),
            P("box", "gen", "neur"),
            P("box", "neur"),
        ),
        check_vma=False,
    )
```

```python
import math

import jax
import jax.numpy as jnp
from jax import lax
from jax.experimental import pallas as pl
from jax.experimental.pallas import tpu as pltpu
from jax.sharding import PartitionSpec as P

MESH = pl.DeviceIdType.MESH
F32 = jnp.float32
BF16 = jnp.bfloat16

NZ = 8
D = 4096
COLS = 512
ROWS = 128
WIDE = 144
NH = 4
PIECE = 256 // NH
HALF = NH // 2
NQ = 4
FQ = COLS // NQ


def neuron(center_pre, radius, phase):
    upper = center_pre + radius
    lower = center_pre - radius
    ratio = jnp.clip(upper / (upper - lower + 1e-05), 0.0, 1.0)
    active = (phase == 1).astype(center_pre.dtype)
    crossing = (phase == 2).astype(center_pre.dtype)
    slope = active + crossing * ratio
    offset = crossing * (-ratio * lower * 0.5)
    return (slope, slope * center_pre + offset, offset)


def zsteps(d):
    return {0: (0,), 4: (4,)}.get(d, (-d, d))


def kernel(
    gens_hbm, center_hbm, w_hbm, bias_hbm, phase_hbm, cot_hbm, ccot_hbm, ocot_hbm,
    cout_ref, gout_ref, off_ref, wg_ref, bg_ref, gg_ref, cg_ref,
    center_ref, bias_ref, phase_ref, ccot_ref, ocot_ref,
    w, wide, acc, cslot, gt, amat, sa, sb, tot, bk, call, sall, xs, cmat, zs, zr, gs, gi, gr, keep, gown, gc, fs, fx, xb,
    load_sem, out_sem, wz_sem, wy_sem, wp_sem, a_sem, s_sem, near_sem, far_sem, pair_sem, f_sem, gx_sem,
):
    me = lax.axis_index("gen")
    x = lax.axis_index("neur")
    yhi = lax.axis_index("box")
    z = me // 4
    ylo = (me // 2) % 2
    c = me % 2
    y = yhi * 2 + ylo
    quad = ylo * 2 + c

    def dev(zz, yy, cc, xx=None):
        return (zz * 4 + (yy % 2) * 2 + cc, x if xx is None else xx, yy // 2)

    def zdev(k, cc=1):
        return dev((z + NZ + k) % NZ, y, cc)

    def ydev(k, cc=1):
        return dev(z, (y + k) % 4, cc)

    def xdev(k, cc):
        return dev(z, y, cc, (x + k) % 4)

    partner = dev(z, y, 1 - c)

    sent = {0: [0, 0, 0, 0], 1: [0, 0, 0, 0]}
    roles = [0, 1]

    def copy_to(src, dst, group, recv_sem, device):
        return pltpu.make_async_remote_copy(
            src_ref=src,
            dst_ref=dst,
            send_sem=out_sem.at[group],
            recv_sem=recv_sem,
            device_id=device,
            device_id_type=MESH,
        )

    def go(src, dst, group, recv_sem, device):
        copy_to(src, dst, group, recv_sem, device).start()
        for role in roles:
            sent[role][group] += math.prod(src.shape) * src.dtype.itemsize

    def await_bytes(ref, recv_sem):
        copy_to(ref, ref, 0, recv_sem, partner).wait_recv()

    barrier = pltpu.get_barrier_semaphore()
    peers = [partner] + [zdev(k, cc) for k in (1, -1) for cc in (0, 1)]
    peers += [f(k, cc) for f in (xdev, ydev) for k in (1, 2, 3) for cc in (0, 1)]
    for peer in peers:
        pl.semaphore_signal(barrier, inc=1, device_id=peer, device_id_type=MESH)

    loads = [
        pltpu.make_async_copy(src, dst, load_sem.at[i])
        for i, (src, dst) in enumerate(
            (
                (gens_hbm, wide.at[pl.ds(0, ROWS)]),
                (center_hbm, center_ref),
                (w_hbm, w.at[pl.ds(pl.multiple_of(me * 128, 128), 128)]),
                (bias_hbm, bias_ref),
                (phase_hbm, phase_ref),
                (cot_hbm, call.at[pl.ds(pl.multiple_of(c * 128, 128), 128)]),
                (ccot_hbm, ccot_ref),
                (ocot_hbm, ocot_ref),
            )
        )
    ]
    for cp in loads:
        cp.start()
    pl.semaphore_wait(barrier, len(peers))

    def chunk(zz, yl, h=0, n=NH):
        at = (zz * 2 + yl) * 256 + h * PIECE
        return w.at[pl.ds(pl.multiple_of(at, PIECE), n * PIECE)]

    for i in range(HALF):
        src = w_hbm.at[i * PIECE : i * PIECE + PIECE]
        for k in (1, -1):
            go(src, chunk(z, ylo, c * HALF + i, 1), 0, wz_sem.at[z, c * HALF + i], zdev(k))
    own_half = chunk(z, ylo, c * HALF, HALF)
    go(w_hbm, own_half, 0, wy_sem.at[z], ydev(1 + 2 * c))
    go(w_hbm, own_half, 0, wp_sem.at[z], partner)

    loads[0].wait()

    def turn(i, carry):
        at = pl.multiple_of((i % 32) * 128, 128)
        gt[pl.ds(at, 128), :] = wide[0:ROWS, pl.ds(at, 128)].astype(F32).T.astype(BF16)
        return carry

    lax.fori_loop(8 * x, 8 * x + 8, turn, 0)
    gt6 = gt.reshape(NZ, 2, 2, 2, 64, 128)

    def lanes(at, n=128):
        return pl.ds(pl.multiple_of(at, 128), n)

    mine = pl.ds(2 * x, 2)
    for k in (2, 1, 3):
        to = (y + k) % 4
        go(
            gt6.at[mine, to % 2, :, to // 2],
            amat.at[mine, :, :, lanes(((4 - k) * 2 + c) * 128)],
            1,
            a_sem.at[0],
            ydev(k),
        )

    loads[1].wait()
    wide[pl.ds(ROWS, 16)] = jnp.concatenate([center_ref[...].astype(F32), jnp.zeros((12, D), F32)], 0).astype(BF16)
    acc[...] = jnp.zeros_like(acc)
    for cp in loads[2:]:
        cp.wait()

    def multiply(zz):
        at = pl.ds(pl.multiple_of(zz * 512, 512), 512)
        res = jnp.dot(wide[:, at], w[at, :], preferred_element_type=F32)
        acc[...] += res[:ROWS]
        cslot[zz] = res[ROWS : ROWS + 8]

    held = (call, sall)

    def part(b, r, cc, n=128):
        return held[b].at[pl.ds(pl.multiple_of((r * 2 + cc) * 128, 128), n)]

    def gather_own(b):
        ref = part(b, 0, c)
        go(ref, part(b, 3, c), 2, near_sem.at[b, c], ydev(1))
        go(ref, part(b, 1, c), 2, near_sem.at[b, 2 + c], ydev(3))
        go(ref, ref, 2, pair_sem.at[b], partner)

    def gather_forward(b):
        for r, cc, to in ((3, 0, 1), (1, 1, 3)):
            await_bytes(part(b, r, cc), near_sem.at[b, cc if r == 3 else 2 + cc])
            go(part(b, r, cc), part(b, 2, cc), 2, far_sem.at[b], ydev(to))

    def sums():
        gen_pre = acc[...]
        cot = part(0, 0, c)[...].astype(F32)
        part_radius = jnp.sum(jnp.abs(gen_pre).reshape(4, 32, COLS), axis=1)
        part_inner = jnp.sum((cot * gen_pre).reshape(4, 32, COLS), axis=1)
        sa[quad] = jnp.concatenate([part_radius, part_inner], 0)

    def signs():
        gen_pre = acc[...]
        sall[pl.ds(pl.multiple_of(c * 128, 128), 128)] = jnp.where(
            gen_pre > 0, 1.0, jnp.where(gen_pre < 0, -1.0, 0.0)
        ).astype(BF16)
        gather_own(1)
        gather_own(0)

    def relax():
        center_pre = cslot[0][0:4]
        for i in range(1, NZ):
            center_pre = center_pre + cslot[i][0:4]
        center_pre = center_pre + bias_ref[...]
        total = tot[...]
        phase = phase_ref[...]
        (slope, center_out, offset), pull = jax.vjp(lambda a, b: neuron(a, b, phase), center_pre, total[0:4])
        g_center, g_radius = pull((total[4:8], ccot_ref[...], ocot_ref[...]))
        return slope, center_out, offset, g_center, g_radius

    def outputs(slope, center_out, offset):
        cout_ref[...] = center_out
        off_ref[...] = offset
        gout_ref[...] = (slope[:, None, :] * acc[...].reshape(4, 32, COLS)).astype(BF16).reshape(ROWS, COLS)

    def centers(g_center):
        center_back = g_center.astype(BF16).astype(F32)
        bias_part = jnp.sum(g_center, axis=0, keepdims=True)
        xb[yhi, :, 0:COLS] = jnp.concatenate([center_back, bias_part, jnp.zeros((3, COLS), F32)], 0)
        chunk_of = jnp.concatenate([center_ref[:, lanes(me * 128)].astype(F32), jnp.zeros((4, 128), F32)], 0)
        xb[yhi, :, COLS:] = jnp.concatenate([chunk_of, jnp.zeros((8, COLS - 128), F32)], 1)
        go(xb.at[yhi], xb.at[yhi], 2, gx_sem.at[1], ydev(2, c))
        return center_back

    other = 1 - yhi

    def center_term():
        await_bytes(xb.at[other], gx_sem.at[1])
        xall = xb[:, :, 0 : COLS + 128].reshape(16, COLS + 128)
        bg_ref[...] = xall[4:5, :COLS] + xall[12:13, :COLS]
        return lax.dot_general(
            xall[:, COLS:].T.astype(BF16), xall[:, :COLS].astype(BF16), (((1,), (0,)), ((), ())), preferred_element_type=F32
        )

    def weight_out(term, count):
        for q in range(NQ):
            await_bytes(fx.at[0:count, q], f_sem.at[q])
            at = q * FQ
            wg_ref[:, at : at + FQ] = fx[:, q].astype(F32).reshape(128, FQ) + term[:, at : at + FQ]

    def drain(role):
        for group, count in enumerate(sent[role]):
            if count:
                ref = w.at[pl.ds(0, count // (COLS * 2))]
                copy_to(ref, ref, group, out_sem.at[group], partner).wait_send()

    @pl.when(c == 0)
    def _():
        roles[:] = [0]
        lax.fori_loop(8 * x + 8, 8 * x + 32, turn, 0)
        go(gt6.at[:, ylo, :, yhi], amat.at[:, :, :, lanes(0)], 1, a_sem.at[2], partner)
        for d in range(5):
            for dz in zsteps(d):
                zz = (z + NZ + dz) % NZ
                await_bytes(w.at[pl.ds(0, 384 if d == 0 else 512)], wp_sem.at[zz])
                multiply(zz)
        sums()
        for to in (partner, dev(z, yhi * 2 + 1 - ylo, 1)):
            go(sa.at[quad], sa.at[quad], 1, s_sem.at[0], to)
        signs()
        await_bytes(tot, s_sem.at[2])
        slope, center_out, offset, g_center, g_radius = relax()
        for b in (0, 1):
            await_bytes(part(b, 0, 1), pair_sem.at[b])
        for cc, at in ((0, 0), (1, 144)):
            cot = part(0, 0, cc)[...].astype(F32).reshape(4, 32, COLS)
            sign = part(1, 0, cc)[...].astype(F32).reshape(4, 32, COLS)
            back = slope[:, None, :] * cot + sign * g_radius[:, None, :]
            bk[at : at + ROWS] = back.astype(BF16).reshape(ROWS, COLS)
        bk[ROWS:144] = jnp.concatenate([centers(g_center), jnp.zeros((12, COLS), F32)], 0).astype(BF16)

        def partial(k):
            at = pl.ds(pl.multiple_of(((x + k) % 4) * 1024, 1024), 1024)
            return lax.dot_general(bk[...], w[at, :], (((1,), (1,)), ((), ())), preferred_element_type=F32)

        first, second = pl.ds(0, 144), pl.ds(144, 128)
        right, left = xdev(1, 0), xdev(3, 0)
        gs[0] = partial(2).astype(BF16)
        go(gs.at[0, first], gi.at[0, first], 2, gx_sem.at[0], right)
        go(gs.at[0, second], gi.at[0, second], 2, gx_sem.at[4], left)
        gown[...] = partial(1)
        gs[1, second] = gown[second].astype(BF16)
        go(gs.at[1, second], gr.at[0, pl.ds(0, 128)], 2, gx_sem.at[5], xdev(1, 1))
        keep[first] = gown[first]
        gown[...] = partial(3)
        gs[2, first] = gown[first].astype(BF16)
        go(gs.at[2, first], gr.at[1], 2, gx_sem.at[5], left)
        keep[second] = gown[second]
        gown[...] = partial(0)
        go(gown.at[second], gown.at[second], 2, gx_sem.at[3], partner)
        await_bytes(gi.at[0, first], gx_sem.at[0])
        gs[1, first] = (keep[first] + gi[0, first].astype(F32)).astype(BF16)
        go(gs.at[1, first], gr.at[0], 2, gx_sem.at[5], right)
        await_bytes(gi.at[0, second], gx_sem.at[4])
        gs[2, second] = (keep[second] + gi[0, second].astype(F32)).astype(BF16)
        go(gs.at[2, second], gr.at[1, pl.ds(0, 128)], 2, gx_sem.at[5], xdev(3, 1))
        outputs(slope, center_out, offset)
        term = center_term()
        await_bytes(gr, gx_sem.at[5])
        summed = gown[first] + gr[0].astype(F32) + gr[1].astype(F32)
        gg_ref[...] = summed[:ROWS]
        cg_ref[...] = summed[ROWS : ROWS + 4]
        gc[...] = summed[ROWS:]
        go(gc, gc, 2, gx_sem.at[0], partner)
        weight_out(term, 2)
        drain(0)

    @pl.when(c == 1)
    def _():
        roles[:] = [1]

        def to_partner(zz, yl):
            go(chunk(zz, yl), chunk(zz, yl), 3, wp_sem.at[zz], partner)

        def handle_y(d):
            for dz in zsteps(d):
                zz = (z + NZ + dz) % NZ
                await_bytes(chunk(zz, 1 - ylo), wy_sem.at[zz])
                to_partner(zz, 1 - ylo)

        def compute(d):
            for dz in zsteps(d):
                multiply((z + NZ + dz) % NZ)

        for d in (1, 2, 3, 4):
            for i in range(NH):
                for way in (0, 1):
                    h = (i + HALF) % NH if way == 0 else i
                    far = (h >= HALF) == (way == 0)
                    if d == 4 and not far:
                        continue
                    zz = (z + NZ - d) % NZ if way == 0 else (z + d) % NZ
                    ref = chunk(zz, ylo, h, 1)
                    await_bytes(ref, wz_sem.at[zz, h])
                    if d < 3 or (d == 3 and far):
                        go(ref, ref, 0, wz_sem.at[zz, h], zdev(1 if way == 0 else -1))
                    to = ydev(1 if h < HALF else 3)
                    if d >= 3:
                        go(ref, ref, 0, wy_sem.at[zz], to)
                    elif i % HALF == HALF - 1:
                        ref = chunk(zz, ylo, 0 if h < HALF else HALF, HALF)
                        go(ref, ref, 0, wy_sem.at[zz], to)
            for dz in zsteps(d):
                to_partner((z + NZ + dz) % NZ, ylo)
            if d >= 2:
                handle_y(d - 2)
            if d == 2:
                await_bytes(chunk(z, ylo, 0, HALF), wp_sem.at[z])
                ref = amat.at[mine, :, :, lanes(256, 768)]
                await_bytes(ref, a_sem.at[0])
                for k in (2, 1, 3):
                    go(ref, ref, 1, a_sem.at[1], xdev(k, 1))
            if d >= 2:
                compute(d - 2)
        handle_y(3)
        compute(3)
        handle_y(4)
        compute(4)

        sums()
        go(sa.at[quad], sa.at[quad], 1, s_sem.at[0], dev(z, yhi * 2 + 1 - ylo, 1))
        signs()
        lax.fori_loop(8 * x + 8, 8 * x + 20, turn, 0)
        await_bytes(sa.at[pl.ds(0, 3)], s_sem.at[0])
        sb[z] = (sa[0] + sa[1]) + (sa[2] + sa[3])
        for k in (4, 3, 5, 2, 6, 1, 7):
            go(sb.at[z], sb.at[z], 1, s_sem.at[1], zdev(k))
        lax.fori_loop(8 * x + 20, 8 * x + 32, turn, 0)
        own_a = pltpu.make_async_copy(gt6.at[:, ylo, :, yhi], amat.at[:, :, :, lanes(128)], load_sem.at[8])
        own_a.start()
        gather_forward(1)
        await_bytes(sb.at[pl.ds(0, NZ - 1)], s_sem.at[1])
        tot[...] = ((sb[0] + sb[1]) + (sb[2] + sb[3])) + ((sb[4] + sb[5]) + (sb[6] + sb[7]))
        go(tot, tot, 1, s_sem.at[2], partner)
        slope, center_out, offset, g_center, g_radius = relax()
        xs[yhi] = jnp.concatenate([slope, g_radius], 0)
        go(xs.at[yhi], xs.at[yhi], 2, gx_sem.at[2], ydev(3 - 2 * ylo))
        gather_forward(0)
        centers(g_center)

        def c_pass(r, box, at, n, first=False):
            cols = pl.ds(at, n)
            rows = pl.ds(pl.multiple_of(r * 256, 256), 256)
            scale = xs[box, 0:4, cols][None, :, None, :]
            g_rad = xs[box, 4:8, cols][None, :, None, :]
            cots = call[rows, cols].astype(F32).reshape(2, 4, 32, n)
            marks = sall[rows, cols].astype(F32).reshape(2, 4, 32, n)
            back = (scale * cots + marks * g_rad).astype(BF16).reshape(256, n)
            a = amat[:, :, :, lanes(r * 256, 256)].reshape(1024, 256)
            res = jnp.dot(a, back, preferred_element_type=F32).reshape(NZ, 128, n)
            if first:
                cmat[:, :, cols] = res
            else:
                cmat[:, :, cols] += res

        def z_step(dist, q):
            for way in (0, 1):
                longest = 4 if q % 2 == way else 3
                if dist > longest:
                    continue
                val = cmat[(z + NZ + (dist if way == 0 else -dist)) % NZ, :, pl.ds(q * FQ, FQ)]
                if dist < longest:
                    await_bytes(zr.at[way, dist, q], wz_sem.at[way * 4 + dist, q])
                    val = val + zr[way, dist, q].astype(F32)
                if dist > 0:
                    zs[way, dist, q] = val.astype(BF16)
                    to = zdev(1 if way == 0 else -1)
                    go(zs.at[way, dist, q], zr.at[way, dist - 1, q], 2, wz_sem.at[way * 4 + dist - 1, q], to)
                elif way == 1:
                    val = val + zr[0, 0, q].astype(F32)
                    fs[q] = val.astype(BF16)
                    fx[yhi, q] = val[64:].astype(BF16)
                    go(fs.at[q, 64:128], fx.at[yhi, q], 2, f_sem.at[q], ydev(2, 1))
                    go(fs.at[q, 0:64], fx.at[yhi, q], 2, f_sem.at[q], ydev(2, 0))
                    go(fs.at[q, 0:64], fx.at[yhi, q], 2, f_sem.at[q], partner)

        own_a.wait()
        await_bytes(amat.at[:, :, :, lanes(0)], a_sem.at[2])
        for b in (0, 1):
            await_bytes(part(b, 0, 0), pair_sem.at[b])
        c_pass(0, yhi, 0, COLS, first=True)
        await_bytes(w.at[pl.ds(0, 1152)], a_sem.at[1])
        for b in (0, 1):
            await_bytes(part(b, 3, 1), near_sem.at[b, 1])
            await_bytes(part(b, 1, 0), near_sem.at[b, 2])
        c_pass(1 + 2 * ylo, yhi, 0, COLS)
        await_bytes(xs.at[other], gx_sem.at[2])
        c_pass(3 - 2 * ylo, other, 0, COLS)
        for b in (0, 1):
            await_bytes(part(b, 2, 0, 256), far_sem.at[b])
        for p in (0, 1):
            c_pass(2, other, p * 256, 256)
            for q in range(p * NQ // 2, (p + 1) * NQ // 2):
                z_step(4, q)
        outputs(slope, center_out, offset)
        for dist in (3, 2, 1, 0):
            if dist == 0:
                term = center_term()
            for q in range(NQ):
                z_step(dist, q)
        second = pl.ds(144, 128)
        await_bytes(gr.at[:, pl.ds(0, 128)], gx_sem.at[5])
        await_bytes(gown.at[second], gx_sem.at[3])
        gg_ref[...] = gown[second] + gr[0, 0:128].astype(F32) + gr[1, 0:128].astype(F32)
        await_bytes(gc, gx_sem.at[0])
        cg_ref[...] = gc[0:4]
        weight_out(term, 1)
        drain(1)


def finish(*refs):
    for src, dst in zip(refs[:7], refs[7:]):
        dst[...] = src[...]


def body(gens, center, weight, bias, phase, gens_cot, center_cot, offset_cot):
    vm = pl.BlockSpec(memory_space=pltpu.VMEM)
    hbm = pl.BlockSpec(memory_space=pltpu.HBM)
    dma = pltpu.SemaphoreType.DMA
    sds = jax.ShapeDtypeStruct
    outs = pl.pallas_call(
        kernel,
        out_shape=(
            sds((4, COLS), F32),
            sds((ROWS, COLS), BF16),
            sds((4, COLS), F32),
            sds((128, COLS), F32),
            sds((1, COLS), F32),
            sds((ROWS, 1024), F32),
            sds((4, 1024), F32),
        ),
        in_specs=[hbm] * 8,
        out_specs=(vm,) * 7,
        scratch_shapes=[
            pltpu.VMEM((4, D), BF16),
            pltpu.VMEM((1, COLS), F32),
            pltpu.VMEM((4, COLS), jnp.int32),
            pltpu.VMEM((4, COLS), F32),
            pltpu.VMEM((4, COLS), F32),
            pltpu.VMEM((D, COLS), BF16),
            pltpu.VMEM((WIDE, D), BF16),
            pltpu.VMEM((ROWS, COLS), F32),
            pltpu.VMEM((NZ, 8, COLS), F32),
            pltpu.VMEM((D, ROWS), BF16),
            pltpu.VMEM((NZ, 2, 64, 1024), BF16),
            pltpu.VMEM((4, 8, COLS), F32),
            pltpu.VMEM((NZ, 8, COLS), F32),
            pltpu.VMEM((8, COLS), F32),
            pltpu.VMEM((272, COLS), BF16),
            pltpu.VMEM((1024, COLS), BF16),
            pltpu.VMEM((1024, COLS), BF16),
            pltpu.VMEM((2, 8, COLS), F32),
            pltpu.VMEM((NZ, 128, COLS), F32),
            pltpu.VMEM((2, 5, NQ, 128, FQ), BF16),
            pltpu.VMEM((2, 5, NQ, 128, FQ), BF16),
            pltpu.VMEM((3, 272, 1024), BF16),
            pltpu.VMEM((1, 272, 1024), BF16),
            pltpu.VMEM((2, 144, 1024), BF16),
            pltpu.VMEM((272, 1024), F32),
            pltpu.VMEM((272, 1024), F32),
            pltpu.VMEM((16, 1024), F32),
            pltpu.VMEM((NQ, 128, FQ), BF16),
            pltpu.VMEM((2, NQ, 64, FQ), BF16),
            pltpu.VMEM((2, 8, 2 * COLS), F32),
            dma((9,)),
            dma((4,)),
            dma((NZ, NH)),
            dma((NZ,)),
            dma((NZ,)),
            dma((3,)),
            dma((3,)),
            dma((2, 4)),
            dma((2,)),
            dma((2,)),
            dma((NQ,)),
            dma((6,)),
        ],
        compiler_params=pltpu.CompilerParams(
            collective_id=0, has_side_effects=True, vmem_limit_bytes=32 * 1024 * 1024
        ),
        name="zonotope_step",
    )(
        *(
            pltpu.with_memory_space_constraint(v, pltpu.HBM)
            for v in (
                gens.reshape(ROWS, D), center, weight, bias.reshape(1, COLS), phase,
                gens_cot.reshape(ROWS, COLS), center_cot, offset_cot,
            )
        )
    )
    outs = pl.pallas_call(
        finish,
        out_shape=tuple(sds(o.shape, o.dtype) for o in outs),
        in_specs=[vm] * 7,
        out_specs=(vm,) * 7,
        compiler_params=pltpu.CompilerParams(vmem_limit_bytes=8 * 1024 * 1024),
        name="finish",
    )(*outs)
    center_out, gens_out, offset, weight_grad, bias_grad, gens_grad, center_grad = outs
    return (
        center_out, gens_out.reshape(4, 32, COLS), offset, weight_grad, bias_grad.reshape(COLS),
        gens_grad.reshape(4, 32, 1024), center_grad,
    )


def solution(mesh):
    return jax.shard_map(
        body,
        mesh=mesh,
        in_specs=(
            P("box", "gen", None),
            P("box", None),
            P("gen", "neur"),
            P("neur"),
            P("box", "neur"),
            P("box", "gen", "neur"),
            P("box", "neur"),
            P("box", "neur"),
        ),
        out_specs=(
            P("box", "neur"),
            P("box", "gen", "neur"),
            P("box", "neur"),
            P("gen", "neur"),
            P("neur"),
            P("box", "gen", "neur"),
            P("box", "neur"),
        ),
        check_vma=False,
    )
```

```python
import math

import jax
import jax.numpy as jnp
from jax import lax
from jax.experimental import pallas as pl
from jax.experimental.pallas import tpu as pltpu
from jax.sharding import PartitionSpec as P

MESH = pl.DeviceIdType.MESH
F32 = jnp.float32
BF16 = jnp.bfloat16

NZ = 8
D = 4096
COLS = 512
ROWS = 128
NH = 4
PIECE = 256 // NH
HALF = NH // 2
NQ = 4
FQ = COLS // NQ


def neuron(center_pre, radius, phase):
    upper = center_pre + radius
    lower = center_pre - radius
    ratio = jnp.clip(upper / (upper - lower + 1e-05), 0.0, 1.0)
    active = (phase == 1).astype(center_pre.dtype)
    crossing = (phase == 2).astype(center_pre.dtype)
    slope = active + crossing * ratio
    offset = crossing * (-ratio * lower * 0.5)
    return (slope, slope * center_pre + offset, offset)


def zsteps(d):
    return {0: (0,), 4: (4,)}.get(d, (-d, d))


def kernel(
    gens_hbm, center_hbm, w_hbm, bias_hbm, phase_hbm, cot_hbm, ccot_hbm, ocot_hbm,
    cout_ref, gout_ref, off_ref, wg_ref, bg_ref, gg_ref, cg_ref,
    center_ref, bias_ref, phase_ref, ccot_ref, ocot_ref,
    w, wide, acc, cslot, gt, amat, sa, sb, tot, bk, call, sall, xs, cmat, zs, zr, gs, gi, gr, keep, gown, gc, fs, fx, xb,
    load_sem, out_sem, wz_sem, wy_sem, wp_sem, a_sem, s_sem, near_sem, far_sem, pair_sem, f_sem, gx_sem,
):
    me = lax.axis_index("gen")
    x = lax.axis_index("neur")
    yhi = lax.axis_index("box")
    z = me // 4
    ylo = (me // 2) % 2
    c = me % 2
    y = yhi * 2 + ylo

    def dev(zz, yy, cc, xx=None):
        return (zz * 4 + (yy % 2) * 2 + cc, x if xx is None else xx, yy // 2)

    def zdev(k, cc=1):
        return dev((z + NZ + k) % NZ, y, cc)

    def ydev(k, cc=1):
        return dev(z, (y + k) % 4, cc)

    def xdev(k, cc):
        return dev(z, y, cc, (x + k) % 4)

    partner = dev(z, y, 1 - c)

    sent = {0: [0, 0, 0, 0], 1: [0, 0, 0, 0]}
    roles = [0, 1]

    def copy_to(src, dst, group, recv_sem, device):
        return pltpu.make_async_remote_copy(
            src_ref=src,
            dst_ref=dst,
            send_sem=out_sem.at[group],
            recv_sem=recv_sem,
            device_id=device,
            device_id_type=MESH,
        )

    def go(src, dst, group, recv_sem, device):
        copy_to(src, dst, group, recv_sem, device).start()
        for role in roles:
            sent[role][group] += math.prod(src.shape) * src.dtype.itemsize

    def await_bytes(ref, recv_sem):
        copy_to(ref, ref, 0, recv_sem, partner).wait_recv()

    barrier = pltpu.get_barrier_semaphore()
    peers = [partner] + [zdev(k, cc) for k in (1, -1) for cc in (0, 1)]
    peers += [f(k, cc) for f in (xdev, ydev) for k in (1, 2, 3) for cc in (0, 1)]
    for peer in peers:
        pl.semaphore_signal(barrier, inc=1, device_id=peer, device_id_type=MESH)

    loads = [
        pltpu.make_async_copy(src, dst, load_sem.at[i])
        for i, (src, dst) in enumerate(
            (
                (gens_hbm, wide.at[pl.ds(pl.multiple_of(c * 144, 16), ROWS)]),
                (center_hbm, center_ref),
                (w_hbm, w.at[pl.ds(pl.multiple_of(me * 128, 128), 128)]),
                (bias_hbm, bias_ref),
                (phase_hbm, phase_ref),
                (cot_hbm, call.at[pl.ds(pl.multiple_of(c * 128, 128), 128)]),
                (ccot_hbm, ccot_ref),
                (ocot_hbm, ocot_ref),
            )
        )
    ]
    for cp in loads:
        cp.start()
    pl.semaphore_wait(barrier, len(peers))

    def chunk(zz, yl, h=0, n=NH):
        at = (zz * 2 + yl) * 256 + h * PIECE
        return w.at[pl.ds(pl.multiple_of(at, PIECE), n * PIECE)]

    for i in range(HALF):
        src = w_hbm.at[i * PIECE : i * PIECE + PIECE]
        for k in (1, -1):
            go(src, chunk(z, ylo, c * HALF + i, 1), 0, wz_sem.at[z, c * HALF + i], zdev(k))
    own_half = chunk(z, ylo, c * HALF, HALF)
    go(w_hbm, own_half, 0, wy_sem.at[z], ydev(1 + 2 * c))
    go(w_hbm, own_half, 0, wp_sem.at[z], partner)

    @pl.when(c == 0)
    def _():
        roles[:] = [0]
        go(gens_hbm, wide.at[pl.ds(0, ROWS)], 3, a_sem.at[3], partner)
        go(cot_hbm, call.at[pl.ds(0, ROWS)], 2, pair_sem.at[0], partner)

    roles[:] = [0, 1]

    loads[0].wait()

    def turn(i, carry):
        at = pl.multiple_of((i % 32) * 128, 128)
        gt[pl.ds(at, 128), :] = wide[pl.ds(pl.multiple_of(c * 144, 16), ROWS), pl.ds(at, 128)].astype(F32).T.astype(BF16)
        return carry

    lax.fori_loop(8 * x, 8 * x + 8, turn, 0)
    gt6 = gt.reshape(NZ, 2, 2, 2, 64, 128)

    def lanes(at, n=128):
        return pl.ds(pl.multiple_of(at, 128), n)

    mine = pl.ds(2 * x, 2)
    for k in (2, 1, 3):
        to = (y + k) % 4
        go(
            gt6.at[mine, to % 2, :, to // 2],
            amat.at[mine, :, :, lanes(((4 - k) * 2 + c) * 128)],
            1,
            a_sem.at[0],
            ydev(k),
        )

    loads[1].wait()
    wide[pl.ds(ROWS, 16)] = jnp.concatenate([center_ref[...].astype(F32), jnp.zeros((12, D), F32)], 0).astype(BF16)
    acc[...] = jnp.zeros_like(acc)
    for cp in loads[2:]:
        cp.wait()

    def multiply(zz, rows):
        at = pl.ds(pl.multiple_of(zz * 512, 512), 512)
        res = jnp.dot(wide[0:rows, at], w[at, :], preferred_element_type=F32)
        acc[0:ROWS] += res[:ROWS]
        if rows > 144:
            acc[ROWS:] += res[144:]
        cslot[zz] = res[ROWS : ROWS + 8]

    held = (call, sall)

    def part(b, r, cc, n=128):
        return held[b].at[pl.ds(pl.multiple_of((r * 2 + cc) * 128, 128), n)]

    def gather_own(b):
        for cc in (0, 1):
            ref = part(b, 0, cc)
            go(ref, part(b, 3, cc), 2, near_sem.at[b, cc], ydev(1))
            go(ref, part(b, 1, cc), 2, near_sem.at[b, 2 + cc], ydev(3))
        go(part(b, 0, 1), part(b, 0, 1), 2, pair_sem.at[b], partner)

    def gather_forward(b):
        for r, cc, to in ((3, 0, 1), (1, 1, 3)):
            await_bytes(part(b, r, cc), near_sem.at[b, cc if r == 3 else 2 + cc])
            go(part(b, r, cc), part(b, 2, cc), 2, far_sem.at[b], ydev(to))

    def signs(n):
        gen_pre = acc[0:n]
        sall[0:n] = jnp.where(gen_pre > 0, 1.0, jnp.where(gen_pre < 0, -1.0, 0.0)).astype(BF16)

    def relax():
        center_pre = cslot[0][0:4]
        for i in range(1, NZ):
            center_pre = center_pre + cslot[i][0:4]
        center_pre = center_pre + bias_ref[...]
        total = tot[...]
        phase = phase_ref[...]
        (slope, center_out, offset), pull = jax.vjp(lambda a, b: neuron(a, b, phase), center_pre, total[0:4])
        g_center, g_radius = pull((total[4:8], ccot_ref[...], ocot_ref[...]))
        return slope, center_out, offset, g_center, g_radius

    def outputs(slope, center_out, offset):
        cout_ref[...] = center_out
        off_ref[...] = offset
        gen_pre = acc[pl.ds(pl.multiple_of(c * ROWS, ROWS), ROWS)].reshape(4, 32, COLS)
        gout_ref[...] = (slope[:, None, :] * gen_pre).astype(BF16).reshape(ROWS, COLS)

    def centers(g_center):
        center_back = g_center.astype(BF16).astype(F32)
        bias_part = jnp.sum(g_center, axis=0, keepdims=True)
        xb[yhi, :, 0:COLS] = jnp.concatenate([center_back, bias_part, jnp.zeros((3, COLS), F32)], 0)
        chunk_of = jnp.concatenate([center_ref[:, lanes(me * 128)].astype(F32), jnp.zeros((4, 128), F32)], 0)
        xb[yhi, :, COLS:] = jnp.concatenate([chunk_of, jnp.zeros((8, COLS - 128), F32)], 1)
        go(xb.at[yhi], xb.at[yhi], 2, gx_sem.at[1], ydev(2, c))
        return center_back

    other = 1 - yhi

    def center_term():
        await_bytes(xb.at[other], gx_sem.at[1])
        xall = xb[:, :, 0 : COLS + 128].reshape(16, COLS + 128)
        bg_ref[...] = xall[4:5, :COLS] + xall[12:13, :COLS]
        return lax.dot_general(
            xall[:, COLS:].T.astype(BF16), xall[:, :COLS].astype(BF16), (((1,), (0,)), ((), ())), preferred_element_type=F32
        )

    def weight_out(term, count):
        for q in range(NQ):
            await_bytes(fx.at[0:count, q], f_sem.at[q])
            at = q * FQ
            wg_ref[:, at : at + FQ] = fx[:, q].astype(F32).reshape(128, FQ) + term[:, at : at + FQ]

    def drain(role):
        for group, count in enumerate(sent[role]):
            if count:
                ref = w.at[pl.ds(0, count // (COLS * 2))]
                copy_to(ref, ref, group, out_sem.at[group], partner).wait_send()

    @pl.when(c == 0)
    def _():
        roles[:] = [0]
        lax.fori_loop(8 * x + 8, 8 * x + 32, turn, 0)
        go(gt6.at[:, ylo, :, yhi], amat.at[:, :, :, lanes(0)], 1, a_sem.at[2], partner)
        for d in range(5):
            for dz in zsteps(d):
                zz = (z + NZ + dz) % NZ
                await_bytes(w.at[pl.ds(0, 384 if d == 0 else 512)], wp_sem.at[zz])
                multiply(zz, 144)
        signs(ROWS)
        await_bytes(tot, s_sem.at[2])
        slope, center_out, offset, g_center, g_radius = relax()
        for b in (0, 1):
            await_bytes(part(b, 0, 1), pair_sem.at[b])
        for cc, at in ((0, 0), (1, 144)):
            cot = part(0, 0, cc)[...].astype(F32).reshape(4, 32, COLS)
            sign = part(1, 0, cc)[...].astype(F32).reshape(4, 32, COLS)
            back = slope[:, None, :] * cot + sign * g_radius[:, None, :]
            bk[at : at + ROWS] = back.astype(BF16).reshape(ROWS, COLS)
        bk[ROWS:144] = jnp.concatenate([centers(g_center), jnp.zeros((12, COLS), F32)], 0).astype(BF16)

        def partial(k):
            at = pl.ds(pl.multiple_of(((x + k) % 4) * 1024, 1024), 1024)
            return lax.dot_general(bk[...], w[at, :], (((1,), (1,)), ((), ())), preferred_element_type=F32)

        first, second = pl.ds(0, 144), pl.ds(144, 128)
        right, left = xdev(1, 0), xdev(3, 0)
        gs[0] = partial(2).astype(BF16)
        go(gs.at[0, first], gi.at[0, first], 2, gx_sem.at[0], right)
        go(gs.at[0, second], gi.at[0, second], 2, gx_sem.at[4], left)
        gown[...] = partial(1)
        gs[1, second] = gown[second].astype(BF16)
        go(gs.at[1, second], gr.at[0, pl.ds(0, 128)], 2, gx_sem.at[5], xdev(1, 1))
        keep[first] = gown[first]
        gown[...] = partial(3)
        gs[2, first] = gown[first].astype(BF16)
        go(gs.at[2, first], gr.at[1], 2, gx_sem.at[5], left)
        keep[second] = gown[second]
        gown[...] = partial(0)
        go(gown.at[second], gown.at[second], 2, gx_sem.at[3], partner)
        await_bytes(gi.at[0, first], gx_sem.at[0])
        gs[1, first] = (keep[first] + gi[0, first].astype(F32)).astype(BF16)
        go(gs.at[1, first], gr.at[0], 2, gx_sem.at[5], right)
        await_bytes(gi.at[0, second], gx_sem.at[4])
        gs[2, second] = (keep[second] + gi[0, second].astype(F32)).astype(BF16)
        go(gs.at[2, second], gr.at[1, pl.ds(0, 128)], 2, gx_sem.at[5], xdev(3, 1))
        outputs(slope, center_out, offset)
        term = center_term()
        await_bytes(gr, gx_sem.at[5])
        summed = gown[first] + gr[0].astype(F32) + gr[1].astype(F32)
        gg_ref[...] = summed[:ROWS]
        cg_ref[...] = summed[ROWS : ROWS + 4]
        gc[...] = summed[ROWS:]
        go(gc, gc, 2, gx_sem.at[0], partner)
        weight_out(term, 2)
        drain(0)

    @pl.when(c == 1)
    def _():
        roles[:] = [1]

        def to_partner(zz, yl):
            go(chunk(zz, yl), chunk(zz, yl), 3, wp_sem.at[zz], partner)

        def handle_y(d):
            for dz in zsteps(d):
                zz = (z + NZ + dz) % NZ
                await_bytes(chunk(zz, 1 - ylo), wy_sem.at[zz])
                to_partner(zz, 1 - ylo)

        def compute(d):
            for dz in zsteps(d):
                multiply((z + NZ + dz) % NZ, 272)

        await_bytes(wide.at[pl.ds(0, ROWS)], a_sem.at[3])
        await_bytes(part(0, 0, 0), pair_sem.at[0])
        for d in (1, 2, 3, 4):
            for i in range(NH):
                for way in (0, 1):
                    h = (i + HALF) % NH if way == 0 else i
                    far = (h >= HALF) == (way == 0)
                    if d == 4 and not far:
                        continue
                    zz = (z + NZ - d) % NZ if way == 0 else (z + d) % NZ
                    ref = chunk(zz, ylo, h, 1)
                    await_bytes(ref, wz_sem.at[zz, h])
                    if d < 3 or (d == 3 and far):
                        go(ref, ref, 0, wz_sem.at[zz, h], zdev(1 if way == 0 else -1))
                    to = ydev(1 if h < HALF else 3)
                    if d >= 3:
                        go(ref, ref, 0, wy_sem.at[zz], to)
                    elif i % HALF == HALF - 1:
                        ref = chunk(zz, ylo, 0 if h < HALF else HALF, HALF)
                        go(ref, ref, 0, wy_sem.at[zz], to)
            for dz in zsteps(d):
                to_partner((z + NZ + dz) % NZ, ylo)
            if d == 4:
                gather_own(0)
            if d >= 2:
                handle_y(d - 2)
            if d == 2:
                await_bytes(chunk(z, ylo, 0, HALF), wp_sem.at[z])
                ref = amat.at[mine, :, :, lanes(256, 768)]
                await_bytes(ref, a_sem.at[0])
                for k in (2, 1, 3):
                    go(ref, ref, 1, a_sem.at[1], xdev(k, 1))
            if d >= 2:
                compute(d - 2)
        handle_y(3)
        compute(3)
        handle_y(4)
        compute(4)

        gen_pre = acc[...].reshape(2, 4, 32, COLS)
        cot = call[0:256].astype(F32).reshape(2, 4, 32, COLS)
        part_radius = jnp.sum(jnp.abs(gen_pre), axis=(0, 2))
        part_inner = jnp.sum(cot * gen_pre, axis=(0, 2))
        sa[ylo] = jnp.concatenate([part_radius, part_inner], 0)
        go(sa.at[ylo], sa.at[ylo], 1, s_sem.at[0], dev(z, yhi * 2 + 1 - ylo, 1))
        signs(256)
        gather_own(1)
        lax.fori_loop(8 * x + 8, 8 * x + 20, turn, 0)
        await_bytes(sa.at[1 - ylo], s_sem.at[0])
        sb[z] = sa[0] + sa[1]
        for k in (4, 3, 5, 2, 6, 1, 7):
            go(sb.at[z], sb.at[z], 1, s_sem.at[1], zdev(k))
        lax.fori_loop(8 * x + 20, 8 * x + 32, turn, 0)
        own_a = pltpu.make_async_copy(gt6.at[:, ylo, :, yhi], amat.at[:, :, :, lanes(128)], load_sem.at[8])
        own_a.start()
        gather_forward(0)
        await_bytes(sb.at[pl.ds(0, NZ - 1)], s_sem.at[1])
        tot[...] = ((sb[0] + sb[1]) + (sb[2] + sb[3])) + ((sb[4] + sb[5]) + (sb[6] + sb[7]))
        go(tot, tot, 1, s_sem.at[2], partner)
        slope, center_out, offset, g_center, g_radius = relax()
        xs[yhi] = jnp.concatenate([slope, g_radius], 0)
        go(xs.at[yhi], xs.at[yhi], 2, gx_sem.at[2], ydev(3 - 2 * ylo))
        gather_forward(1)
        centers(g_center)

        def c_pass(r, box, at, n, first=False):
            cols = pl.ds(at, n)
            rows = pl.ds(pl.multiple_of(r * 256, 256), 256)
            scale = xs[box, 0:4, cols][None, :, None, :]
            g_rad = xs[box, 4:8, cols][None, :, None, :]
            cots = call[rows, cols].astype(F32).reshape(2, 4, 32, n)
            marks = sall[rows, cols].astype(F32).reshape(2, 4, 32, n)
            back = (scale * cots + marks * g_rad).astype(BF16).reshape(256, n)
            a = amat[:, :, :, lanes(r * 256, 256)].reshape(1024, 256)
            res = jnp.dot(a, back, preferred_element_type=F32).reshape(NZ, 128, n)
            if first:
                cmat[:, :, cols] = res
            else:
                cmat[:, :, cols] += res

        def z_step(dist, q):
            for way in (0, 1):
                long = q % 2 == way
                if dist == 4 and not long:
                    continue
                val = cmat[(z + NZ + (dist if way == 0 else -dist)) % NZ, :, pl.ds(q * FQ, FQ)]
                for source in {2: (3, 4) if long else (3,), 1: (2,), 0: (1,)}.get(dist, ()):
                    await_bytes(zr.at[way, source, q], wz_sem.at[way * 4 + source - 1, q])
                    val = val + zr[way, source, q].astype(F32)
                if dist > 0:
                    zs[way, dist, q] = val.astype(BF16)
                    hops = 2 if dist == 4 else 1
                    to = zdev(hops if way == 0 else -hops)
                    go(zs.at[way, dist, q], zr.at[way, dist, q], 2, wz_sem.at[way * 4 + dist - 1, q], to)
                elif way == 0:
                    first = zr[0, 1, q].astype(F32)
                else:
                    val = first + val
                    fs[q] = val.astype(BF16)
                    fx[yhi, q] = val[64:].astype(BF16)
                    go(fs.at[q, 64:128], fx.at[yhi, q], 2, f_sem.at[q], ydev(2, 1))
                    go(fs.at[q, 0:64], fx.at[yhi, q], 2, f_sem.at[q], ydev(2, 0))
                    go(fs.at[q, 0:64], fx.at[yhi, q], 2, f_sem.at[q], partner)

        own_a.wait()
        await_bytes(amat.at[:, :, :, lanes(0)], a_sem.at[2])
        c_pass(0, yhi, 0, COLS, first=True)
        await_bytes(w.at[pl.ds(0, 1152)], a_sem.at[1])
        for b in (0, 1):
            await_bytes(part(b, 3, 1), near_sem.at[b, 1])
            await_bytes(part(b, 1, 0), near_sem.at[b, 2])
        c_pass(1 + 2 * ylo, yhi, 0, COLS)
        await_bytes(xs.at[other], gx_sem.at[2])
        c_pass(3 - 2 * ylo, other, 0, COLS)
        for b in (0, 1):
            await_bytes(part(b, 2, 0, 256), far_sem.at[b])
        for p in (0, 1):
            c_pass(2, other, p * 256, 256)
            for q in range(p * NQ // 2, (p + 1) * NQ // 2):
                z_step(4, q)
                z_step(3, q)
        outputs(slope, center_out, offset)
        for dist in (2, 1, 0):
            if dist == 0:
                term = center_term()
            for q in range(NQ):
                z_step(dist, q)
        second = pl.ds(144, 128)
        await_bytes(gr.at[:, pl.ds(0, 128)], gx_sem.at[5])
        await_bytes(gown.at[second], gx_sem.at[3])
        gg_ref[...] = gown[second] + gr[0, 0:128].astype(F32) + gr[1, 0:128].astype(F32)
        await_bytes(gc, gx_sem.at[0])
        cg_ref[...] = gc[0:4]
        weight_out(term, 1)
        drain(1)


def finish(*refs):
    for src, dst in zip(refs[:7], refs[7:]):
        dst[...] = src[...]


def body(gens, center, weight, bias, phase, gens_cot, center_cot, offset_cot):
    vm = pl.BlockSpec(memory_space=pltpu.VMEM)
    hbm = pl.BlockSpec(memory_space=pltpu.HBM)
    dma = pltpu.SemaphoreType.DMA
    sds = jax.ShapeDtypeStruct
    outs = pl.pallas_call(
        kernel,
        out_shape=(
            sds((4, COLS), F32),
            sds((ROWS, COLS), BF16),
            sds((4, COLS), F32),
            sds((128, COLS), F32),
            sds((1, COLS), F32),
            sds((ROWS, 1024), F32),
            sds((4, 1024), F32),
        ),
        in_specs=[hbm] * 8,
        out_specs=(vm,) * 7,
        scratch_shapes=[
            pltpu.VMEM((4, D), BF16),
            pltpu.VMEM((1, COLS), F32),
            pltpu.VMEM((4, COLS), jnp.int32),
            pltpu.VMEM((4, COLS), F32),
            pltpu.VMEM((4, COLS), F32),
            pltpu.VMEM((D, COLS), BF16),
            pltpu.VMEM((272, D), BF16),
            pltpu.VMEM((2 * ROWS, COLS), F32),
            pltpu.VMEM((NZ, 8, COLS), F32),
            pltpu.VMEM((D, ROWS), BF16),
            pltpu.VMEM((NZ, 2, 64, 1024), BF16),
            pltpu.VMEM((2, 8, COLS), F32),
            pltpu.VMEM((NZ, 8, COLS), F32),
            pltpu.VMEM((8, COLS), F32),
            pltpu.VMEM((272, COLS), BF16),
            pltpu.VMEM((1024, COLS), BF16),
            pltpu.VMEM((1024, COLS), BF16),
            pltpu.VMEM((2, 8, COLS), F32),
            pltpu.VMEM((NZ, 128, COLS), F32),
            pltpu.VMEM((2, 5, NQ, 128, FQ), BF16),
            pltpu.VMEM((2, 5, NQ, 128, FQ), BF16),
            pltpu.VMEM((3, 272, 1024), BF16),
            pltpu.VMEM((1, 272, 1024), BF16),
            pltpu.VMEM((2, 144, 1024), BF16),
            pltpu.VMEM((272, 1024), F32),
            pltpu.VMEM((272, 1024), F32),
            pltpu.VMEM((16, 1024), F32),
            pltpu.VMEM((NQ, 128, FQ), BF16),
            pltpu.VMEM((2, NQ, 64, FQ), BF16),
            pltpu.VMEM((2, 8, 2 * COLS), F32),
            dma((9,)),
            dma((4,)),
            dma((NZ, NH)),
            dma((NZ,)),
            dma((NZ,)),
            dma((4,)),
            dma((3,)),
            dma((2, 4)),
            dma((2,)),
            dma((2,)),
            dma((NQ,)),
            dma((6,)),
        ],
        compiler_params=pltpu.CompilerParams(
            collective_id=0, has_side_effects=True, vmem_limit_bytes=32 * 1024 * 1024
        ),
        name="zonotope_step",
    )(
        *(
            pltpu.with_memory_space_constraint(v, pltpu.HBM)
            for v in (
                gens.reshape(ROWS, D), center, weight, bias.reshape(1, COLS), phase,
                gens_cot.reshape(ROWS, COLS), center_cot, offset_cot,
            )
        )
    )
    outs = pl.pallas_call(
        finish,
        out_shape=tuple(sds(o.shape, o.dtype) for o in outs),
        in_specs=[vm] * 7,
        out_specs=(vm,) * 7,
        compiler_params=pltpu.CompilerParams(vmem_limit_bytes=8 * 1024 * 1024),
        name="finish",
    )(*outs)
    center_out, gens_out, offset, weight_grad, bias_grad, gens_grad, center_grad = outs
    return (
        center_out, gens_out.reshape(4, 32, COLS), offset, weight_grad, bias_grad.reshape(COLS),
        gens_grad.reshape(4, 32, 1024), center_grad,
    )


def solution(mesh):
    return jax.shard_map(
        body,
        mesh=mesh,
        in_specs=(
            P("box", "gen", None),
            P("box", None),
            P("gen", "neur"),
            P("neur"),
            P("box", "neur"),
            P("box", "gen", "neur"),
            P("box", "neur"),
            P("box", "neur"),
        ),
        out_specs=(
            P("box", "neur"),
            P("box", "gen", "neur"),
            P("box", "neur"),
            P("gen", "neur"),
            P("neur"),
            P("box", "gen", "neur"),
            P("box", "neur"),
        ),
        check_vma=False,
    )
```

```python
import math

import jax
import jax.numpy as jnp
from jax import lax
from jax.experimental import pallas as pl
from jax.experimental.pallas import tpu as pltpu
from jax.sharding import PartitionSpec as P

MESH = pl.DeviceIdType.MESH
F32 = jnp.float32
BF16 = jnp.bfloat16

NZ = 8
D = 4096
COLS = 512
ROWS = 128
NH = 4
PIECE = 256 // NH
HALF = NH // 2
NQ = 4
FQ = COLS // NQ


def neuron(center_pre, radius, phase):
    upper = center_pre + radius
    lower = center_pre - radius
    ratio = jnp.clip(upper / (upper - lower + 1e-05), 0.0, 1.0)
    active = (phase == 1).astype(center_pre.dtype)
    crossing = (phase == 2).astype(center_pre.dtype)
    slope = active + crossing * ratio
    offset = crossing * (-ratio * lower * 0.5)
    return (slope, slope * center_pre + offset, offset)


def zsteps(d):
    return {0: (0,), 4: (4,)}.get(d, (-d, d))


def kernel(
    gens_hbm, center_hbm, w_hbm, bias_hbm, phase_hbm, cot_hbm, ccot_hbm, ocot_hbm,
    cout_ref, gout_ref, off_ref, wg_ref, bg_ref, gg_ref, cg_ref,
    center_ref, bias_ref, phase_ref, ccot_ref, ocot_ref,
    w, wide, acc, cslot, gt, amat, sa, sb, tot, bk, call, sall, xs, cmat, zs, zr, gs, gi, gr, keep, gown, gc, fs, fx, xb,
    load_sem, out_sem, wz_sem, wy_sem, wp_sem, a_sem, s_sem, near_sem, far_sem, pair_sem, f_sem, gx_sem,
):
    me = lax.axis_index("gen")
    x = lax.axis_index("neur")
    yhi = lax.axis_index("box")
    z = me // 4
    ylo = (me // 2) % 2
    c = me % 2
    y = yhi * 2 + ylo

    def dev(zz, yy, cc, xx=None):
        return (zz * 4 + (yy % 2) * 2 + cc, x if xx is None else xx, yy // 2)

    def zdev(k, cc=1):
        return dev((z + NZ + k) % NZ, y, cc)

    def ydev(k, cc=1):
        return dev(z, (y + k) % 4, cc)

    def xdev(k, cc):
        return dev(z, y, cc, (x + k) % 4)

    partner = dev(z, y, 1 - c)

    sent = {0: [0, 0, 0, 0], 1: [0, 0, 0, 0]}
    roles = [0, 1]

    def copy_to(src, dst, group, recv_sem, device):
        return pltpu.make_async_remote_copy(
            src_ref=src,
            dst_ref=dst,
            send_sem=out_sem.at[group],
            recv_sem=recv_sem,
            device_id=device,
            device_id_type=MESH,
        )

    def go(src, dst, group, recv_sem, device):
        copy_to(src, dst, group, recv_sem, device).start()
        for role in roles:
            sent[role][group] += math.prod(src.shape) * src.dtype.itemsize

    def await_bytes(ref, recv_sem):
        copy_to(ref, ref, 0, recv_sem, partner).wait_recv()

    barrier = pltpu.get_barrier_semaphore()
    peers = [partner] + [zdev(k, cc) for k in (1, -1) for cc in (0, 1)]
    peers += [f(k, cc) for f in (xdev, ydev) for k in (1, 2, 3) for cc in (0, 1)]
    for peer in peers:
        pl.semaphore_signal(barrier, inc=1, device_id=peer, device_id_type=MESH)

    loads = [
        pltpu.make_async_copy(src, dst, load_sem.at[i])
        for i, (src, dst) in enumerate(
            (
                (gens_hbm, wide.at[pl.ds(pl.multiple_of(c * 144, 16), ROWS)]),
                (center_hbm, center_ref),
                (w_hbm, w.at[pl.ds(pl.multiple_of(me * 128, 128), 128)]),
                (bias_hbm, bias_ref),
                (phase_hbm, phase_ref),
                (cot_hbm, call.at[pl.ds(pl.multiple_of(c * 128, 128), 128)]),
                (ccot_hbm, ccot_ref),
                (ocot_hbm, ocot_ref),
            )
        )
    ]
    for cp in loads:
        cp.start()
    pl.semaphore_wait(barrier, len(peers))

    def chunk(zz, yl, h=0, n=NH):
        at = (zz * 2 + yl) * 256 + h * PIECE
        return w.at[pl.ds(pl.multiple_of(at, PIECE), n * PIECE)]

    for i in range(HALF):
        src = w_hbm.at[i * PIECE : i * PIECE + PIECE]
        for k in (1, -1):
            go(src, chunk(z, ylo, c * HALF + i, 1), 0, wz_sem.at[z, c * HALF + i], zdev(k))
    own_half = chunk(z, ylo, c * HALF, HALF)
    go(w_hbm, own_half, 0, wy_sem.at[z], ydev(1 + 2 * c))
    go(w_hbm, own_half, 0, wp_sem.at[z], partner)

    @pl.when(c == 0)
    def _():
        roles[:] = [0]
        go(gens_hbm, wide.at[pl.ds(0, ROWS)], 3, a_sem.at[3], partner)
        go(cot_hbm, call.at[pl.ds(0, ROWS)], 2, pair_sem.at[0], partner)

    roles[:] = [0, 1]

    loads[0].wait()

    def turn(i, carry):
        at = pl.multiple_of((i % 32) * 128, 128)
        gt[pl.ds(at, 128), :] = wide[pl.ds(pl.multiple_of(c * 144, 16), ROWS), pl.ds(at, 128)].astype(F32).T.astype(BF16)
        return carry

    lax.fori_loop(8 * x, 8 * x + 8, turn, 0)
    gt6 = gt.reshape(NZ, 2, 2, 2, 64, 128)

    def lanes(at, n=128):
        return pl.ds(pl.multiple_of(at, 128), n)

    mine = pl.ds(2 * x, 2)
    for k in (2, 1, 3):
        to = (y + k) % 4
        go(
            gt6.at[mine, to % 2, :, to // 2],
            amat.at[mine, :, :, lanes(((4 - k) * 2 + c) * 128)],
            1,
            a_sem.at[0],
            ydev(k),
        )

    loads[1].wait()
    wide[pl.ds(ROWS, 16)] = jnp.concatenate([center_ref[...].astype(F32), jnp.zeros((12, D), F32)], 0).astype(BF16)
    acc[...] = jnp.zeros_like(acc)
    for cp in loads[2:]:
        cp.wait()

    def multiply(zz, rows):
        at = pl.ds(pl.multiple_of(zz * 512, 512), 512)
        res = jnp.dot(wide[0:rows, at], w[at, :], preferred_element_type=F32)
        acc[0:ROWS] += res[:ROWS]
        if rows > 144:
            acc[ROWS:] += res[144:]
        cslot[zz] = res[ROWS : ROWS + 8]

    held = (call, sall)

    def part(b, r, cc, n=128):
        return held[b].at[pl.ds(pl.multiple_of((r * 2 + cc) * 128, 128), n)]

    def gather_own(b):
        for cc in (0, 1):
            go(part(b, 0, cc), part(b, 3, cc), 2, near_sem.at[b, cc], ydev(1))
            go(part(b, 0, 1 - cc), part(b, 1, 1 - cc), 2, near_sem.at[b, 3 - cc], ydev(3))
        go(part(b, 0, 1), part(b, 0, 1), 2, pair_sem.at[b], partner)

    def gather_forward(b):
        for r, cc, to in ((3, 0, 1), (1, 1, 3)):
            await_bytes(part(b, r, cc), near_sem.at[b, cc if r == 3 else 2 + cc])
            go(part(b, r, cc), part(b, 2, cc), 2, far_sem.at[b], ydev(to))

    def signs(n):
        gen_pre = acc[0:n]
        sall[0:n] = jnp.where(gen_pre > 0, 1.0, jnp.where(gen_pre < 0, -1.0, 0.0)).astype(BF16)

    def relax():
        center_pre = cslot[0][0:4]
        for i in range(1, NZ):
            center_pre = center_pre + cslot[i][0:4]
        center_pre = center_pre + bias_ref[...]
        total = tot[...]
        phase = phase_ref[...]
        (slope, center_out, offset), pull = jax.vjp(lambda a, b: neuron(a, b, phase), center_pre, total[0:4])
        g_center, g_radius = pull((total[4:8], ccot_ref[...], ocot_ref[...]))
        return slope, center_out, offset, g_center, g_radius

    def outputs(slope, center_out, offset):
        cout_ref[...] = center_out
        off_ref[...] = offset
        gen_pre = acc[pl.ds(pl.multiple_of(c * ROWS, ROWS), ROWS)].reshape(4, 32, COLS)
        gout_ref[...] = (slope[:, None, :] * gen_pre).astype(BF16).reshape(ROWS, COLS)

    def centers(g_center):
        center_back = g_center.astype(BF16).astype(F32)
        bias_part = jnp.sum(g_center, axis=0, keepdims=True)
        xb[yhi, :, 0:COLS] = jnp.concatenate([center_back, bias_part, jnp.zeros((3, COLS), F32)], 0)
        chunk_of = jnp.concatenate([center_ref[:, lanes(me * 128)].astype(F32), jnp.zeros((4, 128), F32)], 0)
        xb[yhi, :, COLS:] = jnp.concatenate([chunk_of, jnp.zeros((8, COLS - 128), F32)], 1)
        go(xb.at[yhi], xb.at[yhi], 2, gx_sem.at[1], ydev(2, c))
        return center_back

    other = 1 - yhi

    def center_term():
        await_bytes(xb.at[other], gx_sem.at[1])
        xall = xb[:, :, 0 : COLS + 128].reshape(16, COLS + 128)
        bg_ref[...] = xall[4:5, :COLS] + xall[12:13, :COLS]
        return lax.dot_general(
            xall[:, COLS:].T.astype(BF16), xall[:, :COLS].astype(BF16), (((1,), (0,)), ((), ())), preferred_element_type=F32
        )

    def weight_out(term, count):
        for q in range(NQ):
            await_bytes(fx.at[0:count, q], f_sem.at[q])
            at = q * FQ
            wg_ref[:, at : at + FQ] = fx[:, q].astype(F32).reshape(128, FQ) + term[:, at : at + FQ]

    def drain(role):
        for group, count in enumerate(sent[role]):
            if count:
                ref = w.at[pl.ds(0, count // (COLS * 2))]
                copy_to(ref, ref, group, out_sem.at[group], partner).wait_send()

    @pl.when(c == 0)
    def _():
        roles[:] = [0]
        lax.fori_loop(8 * x + 8, 8 * x + 32, turn, 0)
        go(gt6.at[:, ylo, :, yhi], amat.at[:, :, :, lanes(0)], 1, a_sem.at[2], partner)
        for d in range(5):
            for dz in zsteps(d):
                zz = (z + NZ + dz) % NZ
                await_bytes(w.at[pl.ds(0, 384 if d == 0 else 512)], wp_sem.at[zz])
                multiply(zz, 144)
        signs(ROWS)
        await_bytes(tot, s_sem.at[2])
        slope, center_out, offset, g_center, g_radius = relax()
        for b in (0, 1):
            await_bytes(part(b, 0, 1), pair_sem.at[b])
        for cc, at in ((0, 0), (1, 144)):
            cot = part(0, 0, cc)[...].astype(F32).reshape(4, 32, COLS)
            sign = part(1, 0, cc)[...].astype(F32).reshape(4, 32, COLS)
            back = slope[:, None, :] * cot + sign * g_radius[:, None, :]
            bk[at : at + ROWS] = back.astype(BF16).reshape(ROWS, COLS)
        bk[ROWS:144] = jnp.concatenate([centers(g_center), jnp.zeros((12, COLS), F32)], 0).astype(BF16)

        def partial(k):
            at = pl.ds(pl.multiple_of(((x + k) % 4) * 1024, 1024), 1024)
            return lax.dot_general(bk[...], w[at, :], (((1,), (1,)), ((), ())), preferred_element_type=F32)

        first, second = pl.ds(0, 144), pl.ds(144, 128)
        right, left = xdev(1, 0), xdev(3, 0)
        gs[0] = partial(2).astype(BF16)
        go(gs.at[0, first], gi.at[0, first], 2, gx_sem.at[0], right)
        go(gs.at[0, second], gi.at[0, second], 2, gx_sem.at[4], left)
        gown[...] = partial(1)
        gs[1, second] = gown[second].astype(BF16)
        go(gs.at[1, second], gr.at[0, pl.ds(0, 128)], 2, gx_sem.at[5], xdev(1, 1))
        keep[first] = gown[first]
        gown[...] = partial(3)
        gs[2, first] = gown[first].astype(BF16)
        go(gs.at[2, first], gr.at[1], 2, gx_sem.at[5], left)
        keep[second] = gown[second]
        gown[...] = partial(0)
        go(gown.at[second], gown.at[second], 2, gx_sem.at[3], partner)
        await_bytes(gi.at[0, first], gx_sem.at[0])
        gs[1, first] = (keep[first] + gi[0, first].astype(F32)).astype(BF16)
        go(gs.at[1, first], gr.at[0], 2, gx_sem.at[5], right)
        await_bytes(gi.at[0, second], gx_sem.at[4])
        gs[2, second] = (keep[second] + gi[0, second].astype(F32)).astype(BF16)
        go(gs.at[2, second], gr.at[1, pl.ds(0, 128)], 2, gx_sem.at[5], xdev(3, 1))
        outputs(slope, center_out, offset)
        term = center_term()
        await_bytes(gr, gx_sem.at[5])
        summed = gown[first] + gr[0].astype(F32) + gr[1].astype(F32)
        gg_ref[...] = summed[:ROWS]
        cg_ref[...] = summed[ROWS : ROWS + 4]
        gc[...] = summed[ROWS:]
        go(gc, gc, 2, gx_sem.at[0], partner)
        weight_out(term, 2)
        drain(0)

    @pl.when(c == 1)
    def _():
        roles[:] = [1]

        def to_partner(zz, yl):
            go(chunk(zz, yl), chunk(zz, yl), 3, wp_sem.at[zz], partner)

        def handle_y(d):
            for dz in zsteps(d):
                zz = (z + NZ + dz) % NZ
                await_bytes(chunk(zz, 1 - ylo), wy_sem.at[zz])
                to_partner(zz, 1 - ylo)

        def compute(d):
            for dz in zsteps(d):
                multiply((z + NZ + dz) % NZ, 272)

        for d in (1, 2, 3, 4):
            for i in range(NH):
                for way in (0, 1):
                    h = (i + HALF) % NH if way == 0 else i
                    far = (h >= HALF) == (way == 0)
                    if d == 4 and not far:
                        continue
                    zz = (z + NZ - d) % NZ if way == 0 else (z + d) % NZ
                    ref = chunk(zz, ylo, h, 1)
                    await_bytes(ref, wz_sem.at[zz, h])
                    if d < 3 or (d == 3 and far):
                        go(ref, ref, 0, wz_sem.at[zz, h], zdev(1 if way == 0 else -1))
                    to = ydev(1 if h < HALF else 3)
                    if d >= 3:
                        go(ref, ref, 0, wy_sem.at[zz], to)
                    elif i % HALF == HALF - 1:
                        ref = chunk(zz, ylo, 0 if h < HALF else HALF, HALF)
                        go(ref, ref, 0, wy_sem.at[zz], to)
            for dz in zsteps(d):
                to_partner((z + NZ + dz) % NZ, ylo)
            if d == 4:
                gather_own(0)
            if d >= 2:
                handle_y(d - 2)
            if d == 2:
                await_bytes(chunk(z, ylo, 0, HALF), wp_sem.at[z])
                ref = amat.at[mine, :, :, lanes(256, 768)]
                await_bytes(ref, a_sem.at[0])
                for k in (2, 1, 3):
                    go(ref, ref, 1, a_sem.at[1], xdev(k, 1))
            if d == 3:
                await_bytes(wide.at[pl.ds(0, ROWS)], a_sem.at[3])
                await_bytes(part(0, 0, 0), pair_sem.at[0])
                compute(0)
            if d == 4:
                compute(1)
                compute(2)
        handle_y(3)
        compute(3)
        handle_y(4)
        compute(4)

        gen_pre = acc[...].reshape(2, 4, 32, COLS)
        cot = call[0:256].astype(F32).reshape(2, 4, 32, COLS)
        part_radius = jnp.sum(jnp.abs(gen_pre), axis=(0, 2))
        part_inner = jnp.sum(cot * gen_pre, axis=(0, 2))
        sa[ylo] = jnp.concatenate([part_radius, part_inner], 0)
        go(sa.at[ylo], sa.at[ylo], 1, s_sem.at[0], dev(z, yhi * 2 + 1 - ylo, 1))
        signs(256)
        gather_own(1)
        lax.fori_loop(8 * x + 8, 8 * x + 16, turn, 0)
        await_bytes(sa.at[1 - ylo], s_sem.at[0])
        sb[z] = sa[0] + sa[1]
        for k in (4, 3, 5, 2, 6, 1, 7):
            go(sb.at[z], sb.at[z], 1, s_sem.at[1], zdev(k))
        gather_forward(0)
        lax.fori_loop(8 * x + 16, 8 * x + 32, turn, 0)
        own_a = pltpu.make_async_copy(gt6.at[:, ylo, :, yhi], amat.at[:, :, :, lanes(128)], load_sem.at[8])
        own_a.start()
        gather_forward(1)
        await_bytes(sb.at[pl.ds(0, NZ - 1)], s_sem.at[1])
        tot[...] = ((sb[0] + sb[1]) + (sb[2] + sb[3])) + ((sb[4] + sb[5]) + (sb[6] + sb[7]))
        go(tot, tot, 1, s_sem.at[2], partner)
        slope, center_out, offset, g_center, g_radius = relax()
        xs[yhi] = jnp.concatenate([slope, g_radius], 0)
        go(xs.at[yhi], xs.at[yhi], 2, gx_sem.at[2], ydev(3 - 2 * ylo))
        centers(g_center)

        def c_pass(r, box, at, n, first=False):
            cols = pl.ds(at, n)
            rows = pl.ds(pl.multiple_of(r * 256, 256), 256)
            scale = xs[box, 0:4, cols][None, :, None, :]
            g_rad = xs[box, 4:8, cols][None, :, None, :]
            cots = call[rows, cols].astype(F32).reshape(2, 4, 32, n)
            marks = sall[rows, cols].astype(F32).reshape(2, 4, 32, n)
            back = (scale * cots + marks * g_rad).astype(BF16).reshape(256, n)
            a = amat[:, :, :, lanes(r * 256, 256)].reshape(1024, 256)
            res = jnp.dot(a, back, preferred_element_type=F32).reshape(NZ, 128, n)
            if first:
                cmat[:, :, cols] = res
            else:
                cmat[:, :, cols] += res

        def z_step(dist, q):
            for way in (0, 1):
                long = q % 2 == way
                if dist == 4 and not long:
                    continue
                val = cmat[(z + NZ + (dist if way == 0 else -dist)) % NZ, :, pl.ds(q * FQ, FQ)]
                for source in {2: (3, 4) if long else (3,), 1: (2,), 0: (1,)}.get(dist, ()):
                    await_bytes(zr.at[way, source, q], wz_sem.at[way * 4 + source - 1, q])
                    val = val + zr[way, source, q].astype(F32)
                if dist > 0:
                    zs[way, dist, q] = val.astype(BF16)
                    hops = 2 if dist == 4 else 1
                    to = zdev(hops if way == 0 else -hops)
                    go(zs.at[way, dist, q], zr.at[way, dist, q], 2, wz_sem.at[way * 4 + dist - 1, q], to)
                elif way == 0:
                    first = zr[0, 1, q].astype(F32)
                else:
                    val = first + val
                    fs[q] = val.astype(BF16)
                    fx[yhi, q] = val[64:].astype(BF16)
                    go(fs.at[q, 64:128], fx.at[yhi, q], 2, f_sem.at[q], ydev(2, 1))
                    go(fs.at[q, 0:64], fx.at[yhi, q], 2, f_sem.at[q], ydev(2, 0))
                    go(fs.at[q, 0:64], fx.at[yhi, q], 2, f_sem.at[q], partner)

        own_a.wait()
        await_bytes(amat.at[:, :, :, lanes(0)], a_sem.at[2])
        c_pass(0, yhi, 0, COLS, first=True)
        await_bytes(w.at[pl.ds(0, 1152)], a_sem.at[1])
        for b in (0, 1):
            await_bytes(part(b, 3, 1), near_sem.at[b, 1])
            await_bytes(part(b, 1, 0), near_sem.at[b, 2])
        c_pass(1 + 2 * ylo, yhi, 0, COLS)
        await_bytes(xs.at[other], gx_sem.at[2])
        for b in (0, 1):
            await_bytes(part(b, 2, 0, 256), far_sem.at[b])
        start = 256 * (2 - ylo)
        rows = pl.ds(pl.multiple_of(start, 256), 512)
        scale = xs[other, 0:4][None, :, None, :]
        g_rad = xs[other, 4:8][None, :, None, :]
        cots = call[rows].astype(F32).reshape(4, 4, 32, COLS)
        marks = sall[rows].astype(F32).reshape(4, 4, 32, COLS)
        back = (scale * cots + marks * g_rad).astype(BF16).reshape(512, COLS)

        def block_pass(offsets):
            blocks = [(z + NZ + k) % NZ for k in offsets]
            a = jnp.concatenate([amat[zz, :, :, lanes(start, 512)].reshape(128, 512) for zz in blocks], 0)
            res = jnp.dot(a, back, preferred_element_type=F32)
            for i, zz in enumerate(blocks):
                cmat[zz] += res[i * 128 : i * 128 + 128]

        block_pass((4, 3, -3))
        for q in range(NQ):
            z_step(4, q)
            z_step(3, q)
        block_pass((2, -2, 1, -1, 0))
        outputs(slope, center_out, offset)
        for dist in (2, 1, 0):
            if dist == 0:
                term = center_term()
            for q in range(NQ):
                z_step(dist, q)
        second = pl.ds(144, 128)
        await_bytes(gr.at[:, pl.ds(0, 128)], gx_sem.at[5])
        await_bytes(gown.at[second], gx_sem.at[3])
        gg_ref[...] = gown[second] + gr[0, 0:128].astype(F32) + gr[1, 0:128].astype(F32)
        await_bytes(gc, gx_sem.at[0])
        cg_ref[...] = gc[0:4]
        weight_out(term, 1)
        drain(1)


def finish(*refs):
    for src, dst in zip(refs[:7], refs[7:]):
        dst[...] = src[...]


def body(gens, center, weight, bias, phase, gens_cot, center_cot, offset_cot):
    vm = pl.BlockSpec(memory_space=pltpu.VMEM)
    hbm = pl.BlockSpec(memory_space=pltpu.HBM)
    dma = pltpu.SemaphoreType.DMA
    sds = jax.ShapeDtypeStruct
    outs = pl.pallas_call(
        kernel,
        out_shape=(
            sds((4, COLS), F32),
            sds((ROWS, COLS), BF16),
            sds((4, COLS), F32),
            sds((128, COLS), F32),
            sds((1, COLS), F32),
            sds((ROWS, 1024), F32),
            sds((4, 1024), F32),
        ),
        in_specs=[hbm] * 8,
        out_specs=(vm,) * 7,
        scratch_shapes=[
            pltpu.VMEM((4, D), BF16),
            pltpu.VMEM((1, COLS), F32),
            pltpu.VMEM((4, COLS), jnp.int32),
            pltpu.VMEM((4, COLS), F32),
            pltpu.VMEM((4, COLS), F32),
            pltpu.VMEM((D, COLS), BF16),
            pltpu.VMEM((272, D), BF16),
            pltpu.VMEM((2 * ROWS, COLS), F32),
            pltpu.VMEM((NZ, 8, COLS), F32),
            pltpu.VMEM((D, ROWS), BF16),
            pltpu.VMEM((NZ, 2, 64, 1024), BF16),
            pltpu.VMEM((2, 8, COLS), F32),
            pltpu.VMEM((NZ, 8, COLS), F32),
            pltpu.VMEM((8, COLS), F32),
            pltpu.VMEM((272, COLS), BF16),
            pltpu.VMEM((1024, COLS), BF16),
            pltpu.VMEM((1024, COLS), BF16),
            pltpu.VMEM((2, 8, COLS), F32),
            pltpu.VMEM((NZ, 128, COLS), F32),
            pltpu.VMEM((2, 5, NQ, 128, FQ), BF16),
            pltpu.VMEM((2, 5, NQ, 128, FQ), BF16),
            pltpu.VMEM((3, 272, 1024), BF16),
            pltpu.VMEM((1, 272, 1024), BF16),
            pltpu.VMEM((2, 144, 1024), BF16),
            pltpu.VMEM((272, 1024), F32),
            pltpu.VMEM((272, 1024), F32),
            pltpu.VMEM((16, 1024), F32),
            pltpu.VMEM((NQ, 128, FQ), BF16),
            pltpu.VMEM((2, NQ, 64, FQ), BF16),
            pltpu.VMEM((2, 8, 2 * COLS), F32),
            dma((9,)),
            dma((4,)),
            dma((NZ, NH)),
            dma((NZ,)),
            dma((NZ,)),
            dma((4,)),
            dma((3,)),
            dma((2, 4)),
            dma((2,)),
            dma((2,)),
            dma((NQ,)),
            dma((6,)),
        ],
        compiler_params=pltpu.CompilerParams(
            collective_id=0, has_side_effects=True, vmem_limit_bytes=32 * 1024 * 1024
        ),
        name="zonotope_step",
    )(
        *(
            pltpu.with_memory_space_constraint(v, pltpu.HBM)
            for v in (
                gens.reshape(ROWS, D), center, weight, bias.reshape(1, COLS), phase,
                gens_cot.reshape(ROWS, COLS), center_cot, offset_cot,
            )
        )
    )
    outs = pl.pallas_call(
        finish,
        out_shape=tuple(sds(o.shape, o.dtype) for o in outs),
        in_specs=[vm] * 7,
        out_specs=(vm,) * 7,
        compiler_params=pltpu.CompilerParams(vmem_limit_bytes=8 * 1024 * 1024),
        name="finish",
    )(*outs)
    center_out, gens_out, offset, weight_grad, bias_grad, gens_grad, center_grad = outs
    return (
        center_out, gens_out.reshape(4, 32, COLS), offset, weight_grad, bias_grad.reshape(COLS),
        gens_grad.reshape(4, 32, 1024), center_grad,
    )


def solution(mesh):
    return jax.shard_map(
        body,
        mesh=mesh,
        in_specs=(
            P("box", "gen", None),
            P("box", None),
            P("gen", "neur"),
            P("neur"),
            P("box", "neur"),
            P("box", "gen", "neur"),
            P("box", "neur"),
            P("box", "neur"),
        ),
        out_specs=(
            P("box", "neur"),
            P("box", "gen", "neur"),
            P("box", "neur"),
            P("gen", "neur"),
            P("neur"),
            P("box", "gen", "neur"),
            P("box", "neur"),
        ),
        check_vma=False,
    )
```

```python
import math

import jax
import jax.numpy as jnp
from jax import lax
from jax.experimental import pallas as pl
from jax.experimental.pallas import tpu as pltpu
from jax.sharding import PartitionSpec as P

MESH = pl.DeviceIdType.MESH
F32 = jnp.float32
BF16 = jnp.bfloat16

NZ = 8
D = 4096
COLS = 512
ROWS = 128
NH = 4
PIECE = 256 // NH
HALF = NH // 2
NQ = 4
FQ = COLS // NQ


def neuron(center_pre, radius, phase):
    upper = center_pre + radius
    lower = center_pre - radius
    ratio = jnp.clip(upper / (upper - lower + 1e-05), 0.0, 1.0)
    active = (phase == 1).astype(center_pre.dtype)
    crossing = (phase == 2).astype(center_pre.dtype)
    slope = active + crossing * ratio
    offset = crossing * (-ratio * lower * 0.5)
    return (slope, slope * center_pre + offset, offset)


def zsteps(d):
    return {0: (0,), 4: (4,)}.get(d, (-d, d))


def kernel(
    gens_hbm, center_hbm, w_hbm, bias_hbm, phase_hbm, cot_hbm, ccot_hbm, ocot_hbm,
    cout_ref, gout_ref, off_ref, wg_ref, bg_ref, gg_ref, cg_ref,
    center_ref, bias_ref, phase_ref, ccot_ref, ocot_ref,
    w, wide, acc, cslot, gt, amat, sa, sb, tot, bk, call, sall, xs, cmat, zs, zr, gs, gi, gr, keep, gown, gc, fs, fx, xb,
    load_sem, out_sem, wz_sem, wy_sem, wp_sem, a_sem, s_sem, near_sem, far_sem, pair_sem, f_sem, gx_sem,
):
    me = lax.axis_index("gen")
    x = lax.axis_index("neur")
    yhi = lax.axis_index("box")
    z = me // 4
    ylo = (me // 2) % 2
    c = me % 2
    y = yhi * 2 + ylo

    def dev(zz, yy, cc, xx=None):
        return (zz * 4 + (yy % 2) * 2 + cc, x if xx is None else xx, yy // 2)

    def zdev(k, cc=1):
        return dev((z + NZ + k) % NZ, y, cc)

    def ydev(k, cc=1):
        return dev(z, (y + k) % 4, cc)

    def xdev(k, cc):
        return dev(z, y, cc, (x + k) % 4)

    partner = dev(z, y, 1 - c)

    sent = {0: [0, 0, 0, 0], 1: [0, 0, 0, 0]}
    roles = [0, 1]

    def copy_to(src, dst, group, recv_sem, device):
        return pltpu.make_async_remote_copy(
            src_ref=src,
            dst_ref=dst,
            send_sem=out_sem.at[group],
            recv_sem=recv_sem,
            device_id=device,
            device_id_type=MESH,
        )

    def go(src, dst, group, recv_sem, device):
        copy_to(src, dst, group, recv_sem, device).start()
        for role in roles:
            sent[role][group] += math.prod(src.shape) * src.dtype.itemsize

    def await_bytes(ref, recv_sem):
        copy_to(ref, ref, 0, recv_sem, partner).wait_recv()

    barrier = pltpu.get_barrier_semaphore()
    peers = [partner] + [zdev(k, cc) for k in (1, -1) for cc in (0, 1)]
    peers += [f(k, cc) for f in (xdev, ydev) for k in (1, 2, 3) for cc in (0, 1)]
    for peer in peers:
        pl.semaphore_signal(barrier, inc=1, device_id=peer, device_id_type=MESH)

    loads = [
        pltpu.make_async_copy(src, dst, load_sem.at[i])
        for i, (src, dst) in enumerate(
            (
                (gens_hbm, wide.at[pl.ds(pl.multiple_of(c * 144, 16), ROWS)]),
                (center_hbm, center_ref),
                (w_hbm, w.at[pl.ds(pl.multiple_of(me * 128, 128), 128)]),
                (bias_hbm, bias_ref),
                (phase_hbm, phase_ref),
                (cot_hbm, call.at[pl.ds(pl.multiple_of(c * 128, 128), 128)]),
                (ccot_hbm, ccot_ref),
                (ocot_hbm, ocot_ref),
            )
        )
    ]
    for cp in loads:
        cp.start()
    pl.semaphore_wait(barrier, len(peers))

    def chunk(zz, yl, h=0, n=NH):
        at = (zz * 2 + yl) * 256 + h * PIECE
        return w.at[pl.ds(pl.multiple_of(at, PIECE), n * PIECE)]

    for i in range(HALF):
        src = w_hbm.at[i * PIECE : i * PIECE + PIECE]
        for k in (1, -1):
            go(src, chunk(z, ylo, c * HALF + i, 1), 0, wz_sem.at[z, c * HALF + i], zdev(k))
    own_half = chunk(z, ylo, c * HALF, HALF)
    go(w_hbm, own_half, 0, wy_sem.at[z], ydev(1 + 2 * c))
    go(w_hbm, own_half, 0, wp_sem.at[z], partner)

    @pl.when(c == 0)
    def _():
        roles[:] = [0]
        go(gens_hbm, wide.at[pl.ds(0, ROWS)], 3, a_sem.at[3], partner)
        go(cot_hbm, call.at[pl.ds(0, ROWS)], 2, pair_sem.at[0], partner)

    roles[:] = [0, 1]

    loads[0].wait()

    def turn(i, carry):
        at = pl.multiple_of((i % 32) * 128, 128)
        gt[pl.ds(at, 128), :] = wide[pl.ds(pl.multiple_of(c * 144, 16), ROWS), pl.ds(at, 128)].astype(F32).T.astype(BF16)
        return carry

    lax.fori_loop(8 * x, 8 * x + 8, turn, 0)
    gt6 = gt.reshape(NZ, 2, 2, 2, 64, 128)

    def lanes(at, n=128):
        return pl.ds(pl.multiple_of(at, 128), n)

    mine = pl.ds(2 * x, 2)
    for k in (2, 1, 3):
        to = (y + k) % 4
        go(
            gt6.at[mine, to % 2, :, to // 2],
            amat.at[mine, :, :, lanes(((4 - k) * 2 + c) * 128)],
            1,
            a_sem.at[0],
            ydev(k),
        )

    loads[1].wait()
    wide[pl.ds(ROWS, 16)] = jnp.concatenate([center_ref[...].astype(F32), jnp.zeros((12, D), F32)], 0).astype(BF16)
    acc[...] = jnp.zeros_like(acc)
    for cp in loads[2:]:
        cp.wait()

    def multiply(zz, rows):
        at = pl.ds(pl.multiple_of(zz * 512, 512), 512)
        res = jnp.dot(wide[0:rows, at], w[at, :], preferred_element_type=F32)
        acc[0:ROWS] += res[:ROWS]
        if rows > 144:
            acc[ROWS:] += res[144:]
        cslot[zz] = res[ROWS : ROWS + 8]

    held = (call, sall)

    def part(b, r, cc, n=128):
        return held[b].at[pl.ds(pl.multiple_of((r * 2 + cc) * 128, 128), n)]

    def gather_own(b):
        for cc in (0, 1):
            go(part(b, 0, cc), part(b, 3, cc), 2, near_sem.at[b, cc], ydev(1))
            go(part(b, 0, 1 - cc), part(b, 1, 1 - cc), 2, near_sem.at[b, 3 - cc], ydev(3))
        go(part(b, 0, 1), part(b, 0, 1), 2, pair_sem.at[b], partner)

    def gather_forward(b):
        for r, cc, to in ((3, 0, 1), (1, 1, 3)):
            await_bytes(part(b, r, cc), near_sem.at[b, cc if r == 3 else 2 + cc])
            go(part(b, r, cc), part(b, 2, cc), 2, far_sem.at[b], ydev(to))

    def signs(n):
        gen_pre = acc[0:n]
        sall[0:n] = jnp.where(gen_pre > 0, 1.0, jnp.where(gen_pre < 0, -1.0, 0.0)).astype(BF16)

    def relax():
        center_pre = cslot[0][0:4]
        for i in range(1, NZ):
            center_pre = center_pre + cslot[i][0:4]
        center_pre = center_pre + bias_ref[...]
        total = tot[...]
        phase = phase_ref[...]
        (slope, center_out, offset), pull = jax.vjp(lambda a, b: neuron(a, b, phase), center_pre, total[0:4])
        g_center, g_radius = pull((total[4:8], ccot_ref[...], ocot_ref[...]))
        return slope, center_out, offset, g_center, g_radius

    def outputs(slope, center_out, offset):
        cout_ref[...] = center_out
        off_ref[...] = offset
        gen_pre = acc[pl.ds(pl.multiple_of(c * ROWS, ROWS), ROWS)].reshape(4, 32, COLS)
        gout_ref[...] = (slope[:, None, :] * gen_pre).astype(BF16).reshape(ROWS, COLS)

    def centers(g_center):
        center_back = g_center.astype(BF16).astype(F32)
        bias_part = jnp.sum(g_center, axis=0, keepdims=True)
        xb[yhi, :, 0:COLS] = jnp.concatenate([center_back, bias_part, jnp.zeros((3, COLS), F32)], 0)
        chunk_of = jnp.concatenate([center_ref[:, lanes(me * 128)].astype(F32), jnp.zeros((4, 128), F32)], 0)
        xb[yhi, :, COLS:] = jnp.concatenate([chunk_of, jnp.zeros((8, COLS - 128), F32)], 1)
        go(xb.at[yhi], xb.at[yhi], 2, gx_sem.at[1], ydev(2, c))
        return center_back

    other = 1 - yhi

    def center_term():
        await_bytes(xb.at[other], gx_sem.at[1])
        xall = xb[:, :, 0 : COLS + 128].reshape(16, COLS + 128)
        bg_ref[...] = xall[4:5, :COLS] + xall[12:13, :COLS]
        return lax.dot_general(
            xall[:, COLS:].T.astype(BF16), xall[:, :COLS].astype(BF16), (((1,), (0,)), ((), ())), preferred_element_type=F32
        )

    def weight_out(term, count):
        for q in range(NQ):
            await_bytes(fx.at[0:count, q], f_sem.at[q])
            at = q * FQ
            wg_ref[:, at : at + FQ] = fx[:, q].astype(F32).reshape(128, FQ) + term[:, at : at + FQ]

    def drain(role):
        for group, count in enumerate(sent[role]):
            if count:
                ref = w.at[pl.ds(0, count // (COLS * 2))]
                copy_to(ref, ref, group, out_sem.at[group], partner).wait_send()

    @pl.when(c == 0)
    def _():
        roles[:] = [0]
        lax.fori_loop(8 * x + 8, 8 * x + 32, turn, 0)
        go(gt6.at[:, ylo, :, yhi], amat.at[:, :, :, lanes(0)], 1, a_sem.at[2], partner)
        for d in range(5):
            for dz in zsteps(d):
                zz = (z + NZ + dz) % NZ
                await_bytes(w.at[pl.ds(0, 384 if d == 0 else 512)], wp_sem.at[zz])
                multiply(zz, 144)
        signs(ROWS)
        await_bytes(tot, s_sem.at[2])
        slope, center_out, offset, g_center, g_radius = relax()
        for b in (0, 1):
            await_bytes(part(b, 0, 1), pair_sem.at[b])
        for cc, at in ((0, 0), (1, 144)):
            cot = part(0, 0, cc)[...].astype(F32).reshape(4, 32, COLS)
            sign = part(1, 0, cc)[...].astype(F32).reshape(4, 32, COLS)
            back = slope[:, None, :] * cot + sign * g_radius[:, None, :]
            bk[at : at + ROWS] = back.astype(BF16).reshape(ROWS, COLS)
        bk[ROWS:144] = jnp.concatenate([centers(g_center), jnp.zeros((12, COLS), F32)], 0).astype(BF16)

        def partial(k):
            at = pl.ds(pl.multiple_of(((x + k) % 4) * 1024, 1024), 1024)
            return lax.dot_general(bk[...], w[at, :], (((1,), (1,)), ((), ())), preferred_element_type=F32)

        first, second = pl.ds(0, 144), pl.ds(144, 128)
        right, left = xdev(1, 0), xdev(3, 0)
        gs[0] = partial(2).astype(BF16)
        go(gs.at[0, first], gi.at[0, first], 2, gx_sem.at[0], right)
        go(gs.at[0, second], gi.at[0, second], 2, gx_sem.at[4], left)
        gown[...] = partial(1)
        gs[1, second] = gown[second].astype(BF16)
        go(gs.at[1, second], gr.at[0, pl.ds(0, 128)], 2, gx_sem.at[5], xdev(1, 1))
        keep[first] = gown[first]
        gown[...] = partial(3)
        gs[2, first] = gown[first].astype(BF16)
        go(gs.at[2, first], gr.at[1], 2, gx_sem.at[5], left)
        keep[second] = gown[second]
        gown[...] = partial(0)
        go(gown.at[second], gown.at[second], 2, gx_sem.at[3], partner)
        await_bytes(gi.at[0, first], gx_sem.at[0])
        gs[1, first] = (keep[first] + gi[0, first].astype(F32)).astype(BF16)
        go(gs.at[1, first], gr.at[0], 2, gx_sem.at[5], right)
        await_bytes(gi.at[0, second], gx_sem.at[4])
        gs[2, second] = (keep[second] + gi[0, second].astype(F32)).astype(BF16)
        go(gs.at[2, second], gr.at[1, pl.ds(0, 128)], 2, gx_sem.at[5], xdev(3, 1))
        outputs(slope, center_out, offset)
        term = center_term()
        await_bytes(gr, gx_sem.at[5])
        summed = gown[first] + gr[0].astype(F32) + gr[1].astype(F32)
        gg_ref[...] = summed[:ROWS]
        cg_ref[...] = summed[ROWS : ROWS + 4]
        gc[...] = summed[ROWS:]
        go(gc, gc, 2, gx_sem.at[0], partner)
        weight_out(term, 2)
        drain(0)

    @pl.when(c == 1)
    def _():
        roles[:] = [1]

        def to_partner(zz, yl):
            go(chunk(zz, yl), chunk(zz, yl), 3, wp_sem.at[zz], partner)

        def handle_y(d):
            for dz in zsteps(d):
                zz = (z + NZ + dz) % NZ
                await_bytes(chunk(zz, 1 - ylo), wy_sem.at[zz])
                to_partner(zz, 1 - ylo)

        def compute(d):
            for dz in zsteps(d):
                multiply((z + NZ + dz) % NZ, 272)

        for d in (1, 2, 3, 4):
            for i in range(NH):
                for way in (0, 1):
                    h = (i + HALF) % NH if way == 0 else i
                    far = (h >= HALF) == (way == 0)
                    if d == 4 and not far:
                        continue
                    zz = (z + NZ - d) % NZ if way == 0 else (z + d) % NZ
                    ref = chunk(zz, ylo, h, 1)
                    await_bytes(ref, wz_sem.at[zz, h])
                    if d < 3 or (d == 3 and far):
                        go(ref, ref, 0, wz_sem.at[zz, h], zdev(1 if way == 0 else -1))
                    to = ydev(1 if h < HALF else 3)
                    go(ref, ref, 0, wy_sem.at[zz], to)
            for dz in zsteps(d):
                to_partner((z + NZ + dz) % NZ, ylo)
            if d == 4:
                gather_own(0)
            if d >= 2:
                handle_y(d - 2)
            if d == 2:
                await_bytes(chunk(z, ylo, 0, HALF), wp_sem.at[z])
                ref = amat.at[mine, :, :, lanes(256, 768)]
                await_bytes(ref, a_sem.at[0])
                for k in (2, 1, 3):
                    go(ref, ref, 1, a_sem.at[1], xdev(k, 1))
            if d == 3:
                await_bytes(wide.at[pl.ds(0, ROWS)], a_sem.at[3])
                await_bytes(part(0, 0, 0), pair_sem.at[0])
                compute(0)
            if d == 4:
                compute(1)
                compute(2)
        handle_y(3)
        compute(3)
        handle_y(4)
        compute(4)

        gen_pre = acc[...].reshape(2, 4, 32, COLS)
        cot = call[0:256].astype(F32).reshape(2, 4, 32, COLS)
        part_radius = jnp.sum(jnp.abs(gen_pre), axis=(0, 2))
        part_inner = jnp.sum(cot * gen_pre, axis=(0, 2))
        sa[ylo] = jnp.concatenate([part_radius, part_inner], 0)
        go(sa.at[ylo], sa.at[ylo], 1, s_sem.at[0], dev(z, yhi * 2 + 1 - ylo, 1))
        signs(256)
        gather_own(1)
        await_bytes(sa.at[1 - ylo], s_sem.at[0])
        sb[z] = sa[0] + sa[1]
        for k in (4, 3, 5, 2, 6, 1, 7):
            go(sb.at[z], sb.at[z], 1, s_sem.at[1], zdev(k))
        gather_forward(0)
        lax.fori_loop(8 * x + 8, 8 * x + 32, turn, 0)
        own_a = pltpu.make_async_copy(gt6.at[:, ylo, :, yhi], amat.at[:, :, :, lanes(128)], load_sem.at[8])
        own_a.start()
        gather_forward(1)
        await_bytes(sb.at[pl.ds(0, NZ - 1)], s_sem.at[1])
        tot[...] = ((sb[0] + sb[1]) + (sb[2] + sb[3])) + ((sb[4] + sb[5]) + (sb[6] + sb[7]))
        go(tot, tot, 1, s_sem.at[2], partner)
        slope, center_out, offset, g_center, g_radius = relax()
        xs[yhi] = jnp.concatenate([slope, g_radius], 0)
        go(xs.at[yhi], xs.at[yhi], 2, gx_sem.at[2], ydev(3 - 2 * ylo))
        centers(g_center)

        def c_pass(r, box, at, n, first=False):
            cols = pl.ds(at, n)
            rows = pl.ds(pl.multiple_of(r * 256, 256), 256)
            scale = xs[box, 0:4, cols][None, :, None, :]
            g_rad = xs[box, 4:8, cols][None, :, None, :]
            cots = call[rows, cols].astype(F32).reshape(2, 4, 32, n)
            marks = sall[rows, cols].astype(F32).reshape(2, 4, 32, n)
            back = (scale * cots + marks * g_rad).astype(BF16).reshape(256, n)
            a = amat[:, :, :, lanes(r * 256, 256)].reshape(1024, 256)
            res = jnp.dot(a, back, preferred_element_type=F32).reshape(NZ, 128, n)
            if first:
                cmat[:, :, cols] = res
            else:
                cmat[:, :, cols] += res

        def z_step(dist, q):
            for way in (0, 1):
                long = q % 2 == way
                if dist == 4 and not long:
                    continue
                val = cmat[(z + NZ + (dist if way == 0 else -dist)) % NZ, :, pl.ds(q * FQ, FQ)]
                for source in {2: (3, 4) if long else (3,), 1: (2,), 0: (1,)}.get(dist, ()):
                    await_bytes(zr.at[way, source, q], wz_sem.at[way * 4 + source - 1, q])
                    val = val + zr[way, source, q].astype(F32)
                if dist > 0:
                    zs[way, dist, q] = val.astype(BF16)
                    hops = 2 if dist == 4 else 1
                    to = zdev(hops if way == 0 else -hops)
                    go(zs.at[way, dist, q], zr.at[way, dist, q], 2, wz_sem.at[way * 4 + dist - 1, q], to)
                elif way == 0:
                    first = zr[0, 1, q].astype(F32)
                else:
                    val = first + val
                    fs[q] = val.astype(BF16)
                    fx[yhi, q] = val[64:].astype(BF16)
                    go(fs.at[q, 64:128], fx.at[yhi, q], 2, f_sem.at[q], ydev(2, 1))
                    go(fs.at[q, 0:64], fx.at[yhi, q], 2, f_sem.at[q], ydev(2, 0))
                    go(fs.at[q, 0:64], fx.at[yhi, q], 2, f_sem.at[q], partner)

        own_a.wait()
        await_bytes(amat.at[:, :, :, lanes(0)], a_sem.at[2])
        c_pass(0, yhi, 0, COLS, first=True)
        await_bytes(w.at[pl.ds(0, 1152)], a_sem.at[1])
        for b in (0, 1):
            await_bytes(part(b, 3, 1), near_sem.at[b, 1])
            await_bytes(part(b, 1, 0), near_sem.at[b, 2])
        c_pass(1 + 2 * ylo, yhi, 0, COLS)
        await_bytes(xs.at[other], gx_sem.at[2])
        for b in (0, 1):
            await_bytes(part(b, 2, 0, 256), far_sem.at[b])
        start = 256 * (2 - ylo)
        rows = pl.ds(pl.multiple_of(start, 256), 512)
        scale = xs[other, 0:4][None, :, None, :]
        g_rad = xs[other, 4:8][None, :, None, :]
        cots = call[rows].astype(F32).reshape(4, 4, 32, COLS)
        marks = sall[rows].astype(F32).reshape(4, 4, 32, COLS)
        back = (scale * cots + marks * g_rad).astype(BF16).reshape(512, COLS)

        def block_pass(offsets):
            blocks = [(z + NZ + k) % NZ for k in offsets]
            a = jnp.concatenate([amat[zz, :, :, lanes(start, 512)].reshape(128, 512) for zz in blocks], 0)
            res = jnp.dot(a, back, preferred_element_type=F32)
            for i, zz in enumerate(blocks):
                cmat[zz] += res[i * 128 : i * 128 + 128]

        block_pass((4, 3, -3))
        for q in range(NQ):
            z_step(4, q)
            z_step(3, q)
        block_pass((2, -2, 1, -1, 0))
        outputs(slope, center_out, offset)
        for dist in (2, 1, 0):
            if dist == 0:
                term = center_term()
            for q in range(NQ):
                z_step(dist, q)
        second = pl.ds(144, 128)
        await_bytes(gr.at[:, pl.ds(0, 128)], gx_sem.at[5])
        await_bytes(gown.at[second], gx_sem.at[3])
        gg_ref[...] = gown[second] + gr[0, 0:128].astype(F32) + gr[1, 0:128].astype(F32)
        await_bytes(gc, gx_sem.at[0])
        cg_ref[...] = gc[0:4]
        weight_out(term, 1)
        drain(1)


def finish(*refs):
    for src, dst in zip(refs[:7], refs[7:]):
        dst[...] = src[...]


def body(gens, center, weight, bias, phase, gens_cot, center_cot, offset_cot):
    vm = pl.BlockSpec(memory_space=pltpu.VMEM)
    hbm = pl.BlockSpec(memory_space=pltpu.HBM)
    dma = pltpu.SemaphoreType.DMA
    sds = jax.ShapeDtypeStruct
    outs = pl.pallas_call(
        kernel,
        out_shape=(
            sds((4, COLS), F32),
            sds((ROWS, COLS), BF16),
            sds((4, COLS), F32),
            sds((128, COLS), F32),
            sds((1, COLS), F32),
            sds((ROWS, 1024), F32),
            sds((4, 1024), F32),
        ),
        in_specs=[hbm] * 8,
        out_specs=(vm,) * 7,
        scratch_shapes=[
            pltpu.VMEM((4, D), BF16),
            pltpu.VMEM((1, COLS), F32),
            pltpu.VMEM((4, COLS), jnp.int32),
            pltpu.VMEM((4, COLS), F32),
            pltpu.VMEM((4, COLS), F32),
            pltpu.VMEM((D, COLS), BF16),
            pltpu.VMEM((272, D), BF16),
            pltpu.VMEM((2 * ROWS, COLS), F32),
            pltpu.VMEM((NZ, 8, COLS), F32),
            pltpu.VMEM((D, ROWS), BF16),
            pltpu.VMEM((NZ, 2, 64, 1024), BF16),
            pltpu.VMEM((2, 8, COLS), F32),
            pltpu.VMEM((NZ, 8, COLS), F32),
            pltpu.VMEM((8, COLS), F32),
            pltpu.VMEM((272, COLS), BF16),
            pltpu.VMEM((1024, COLS), BF16),
            pltpu.VMEM((1024, COLS), BF16),
            pltpu.VMEM((2, 8, COLS), F32),
            pltpu.VMEM((NZ, 128, COLS), F32),
            pltpu.VMEM((2, 5, NQ, 128, FQ), BF16),
            pltpu.VMEM((2, 5, NQ, 128, FQ), BF16),
            pltpu.VMEM((3, 272, 1024), BF16),
            pltpu.VMEM((1, 272, 1024), BF16),
            pltpu.VMEM((2, 144, 1024), BF16),
            pltpu.VMEM((272, 1024), F32),
            pltpu.VMEM((272, 1024), F32),
            pltpu.VMEM((16, 1024), F32),
            pltpu.VMEM((NQ, 128, FQ), BF16),
            pltpu.VMEM((2, NQ, 64, FQ), BF16),
            pltpu.VMEM((2, 8, 2 * COLS), F32),
            dma((9,)),
            dma((4,)),
            dma((NZ, NH)),
            dma((NZ,)),
            dma((NZ,)),
            dma((4,)),
            dma((3,)),
            dma((2, 4)),
            dma((2,)),
            dma((2,)),
            dma((NQ,)),
            dma((6,)),
        ],
        compiler_params=pltpu.CompilerParams(
            collective_id=0, has_side_effects=True, vmem_limit_bytes=32 * 1024 * 1024
        ),
        name="zonotope_step",
    )(
        *(
            pltpu.with_memory_space_constraint(v, pltpu.HBM)
            for v in (
                gens.reshape(ROWS, D), center, weight, bias.reshape(1, COLS), phase,
                gens_cot.reshape(ROWS, COLS), center_cot, offset_cot,
            )
        )
    )
    outs = pl.pallas_call(
        finish,
        out_shape=tuple(sds(o.shape, o.dtype) for o in outs),
        in_specs=[vm] * 7,
        out_specs=(vm,) * 7,
        compiler_params=pltpu.CompilerParams(vmem_limit_bytes=8 * 1024 * 1024),
        name="finish",
    )(*outs)
    center_out, gens_out, offset, weight_grad, bias_grad, gens_grad, center_grad = outs
    return (
        center_out, gens_out.reshape(4, 32, COLS), offset, weight_grad, bias_grad.reshape(COLS),
        gens_grad.reshape(4, 32, 1024), center_grad,
    )


def solution(mesh):
    return jax.shard_map(
        body,
        mesh=mesh,
        in_specs=(
            P("box", "gen", None),
            P("box", None),
            P("gen", "neur"),
            P("neur"),
            P("box", "neur"),
            P("box", "gen", "neur"),
            P("box", "neur"),
            P("box", "neur"),
        ),
        out_specs=(
            P("box", "neur"),
            P("box", "gen", "neur"),
            P("box", "neur"),
            P("gen", "neur"),
            P("neur"),
            P("box", "gen", "neur"),
            P("box", "neur"),
        ),
        check_vma=False,
    )
```
